512 devices in a mesh: src: 128 (over y, z, core), depth: 4 (over x).
Axes of the slice: x: 4, y: 8, z: 8, core: 2. Of those that a mesh axis runs over, the one named last changes fastest.
Arguments:
- incident: float32 [128, 4, 2, 4096], P('src'), may hold values from -6 to 6
- encode: int32 [128], P('src'), may hold values from 0 to 15
- freq_index: int32 [128], P('src'), may hold values from 0 to 7
- wavenum: float32 [8], replicated, may hold values from 1 to 2.8
- slowness: float32 [4, 4096], P('depth'), may hold values from -6 to 6
- probes: bfloat16 [64, 4, 4096], P(None, 'depth'), may hold values from -6 to 6
Outputs:
- sketch_basis: float32 [64, 4, 4096], P(None, 'depth', 'src')
- r_factor: float32 [64, 64], replicated
The draws below stay inside these ranges and needn't reach their ends.
All inputs are finite; a program needn't handle non-finite values.
Results may differ from the reference program's by a relative error of at most 0.02.
Values may be sent and summed in bfloat16 or wider, within the bound.
A program may use at most 128 MiB of HBM per device.

```python
import math
import jax
import jax.numpy as jnp
from jax import lax

SIDE = 64
NXL = 4096
PROBES = 64
NSRC = 4
NF = 8
PLANES = 4
GROUPS = 128


def plant(drawn, rng, smallest, top_value):
    longest = drawn.shape.index(max(drawn.shape))
    spots = []
    for shift in (0, 1):
        where = [jax.random.randint(jax.random.fold_in(rng, axis), (), 0, length) for axis, length in enumerate(drawn.shape)]
        where[longest] = (where[longest] + shift) % drawn.shape[longest]
        spots.append(tuple(where))
    return drawn.at[spots[0]].set(smallest).at[spots[1]].set(top_value)


def with_spikes(drawn, key, source, target, blocks, factor):
    def block_of(dim):
        return (jnp.arange(drawn.shape[dim]) // (drawn.shape[dim] // blocks)).reshape((-1,) + (1,) * (drawn.ndim - 1 - dim))

    near = jax.random.permutation(key, blocks)[block_of(target)]
    second = (block_of(target) + blocks // 2) % blocks
    return jnp.where((block_of(source) == near) | (block_of(source) == second), factor * drawn, drawn)


def steps_of(key, shape, split, low, top_value):
    def one(dim, shards_of):
        steps = jax.random.uniform(jax.random.fold_in(jax.random.fold_in(key, 6), dim), (shards_of,), jnp.float32, low / len(split), top_value / len(split))
        return jnp.repeat(jnp.exp(steps), shape[dim] // shards_of).reshape((-1,) + (1,) * (len(shape) - dim - 1))

    level = one(*split[0])
    for cut in split[1:]:
        level = level * one(*cut)
    return level


def centred(key, shape, deviation, limit, pieces=(), kind=jnp.bfloat16):
    values = jax.random.normal(key, shape, jnp.float32) * deviation
    if len(pieces) > 0:
        values = steps_of(key, shape, pieces, -0.22, 0.18) * values
    return jnp.clip(values, min=-limit, max=limit).astype(kind)


def bell_draw_with(stream_key, extent, deviation, bound, pieces, heavy, kind=jnp.bfloat16):
    entries = deviation * jax.random.normal(stream_key, extent, jnp.float32)
    if pieces:
        entries = entries * steps_of(stream_key, extent, pieces, -0.22, 0.18)
    return jnp.clip(with_spikes(entries, jax.random.fold_in(stream_key, 3), *heavy), -bound, bound).astype(kind)


def setup_inputs(seed: int = 0) -> dict:
    key_of = jax.random.split(jax.random.key(seed), 7)
    incident = bell_draw_with(key_of[0], (GROUPS, NSRC, 2, NXL), 0.5, 6.0, ((0, 128),), (0, 3, 128, 5.5), jnp.float32)
    encode = plant(jax.random.randint(key_of[1], (GROUPS,), 0, 2 ** NSRC), jax.random.fold_in(key_of[1], 1), 0, (2 ** NSRC) - 1).astype(jnp.int32)
    freq_index = plant(jax.random.randint(key_of[2], (GROUPS,), 0, NF), jax.random.fold_in(key_of[2], 1), 0, NF - 1).astype(jnp.int32)
    wavenum = jnp.clip(jnp.exp(jax.random.uniform(key_of[3], (NF,), jnp.float32, math.log(1.0), math.log(2.8))), 1.0, 2.8)
    slowness = centred(key_of[4], (PLANES, NXL), 0.5, 6.0, ((0, 4),), jnp.float32)
    probes = centred(key_of[5], (PROBES, PLANES, NXL), 1.0, 6.0, ((1, 4),))
    return {"incident": incident, "encode": encode, "freq_index": freq_index, "wavenum": wavenum, "slowness": slowness, "probes": probes}


DAMPING = 0.5
STEP_DEPTH = 1.0

def dft_tables(points, direction):
    counter = jnp.arange(points, dtype=jnp.int32)
    product = counter[:, None] * counter[None, :] % points
    angles = 2.0 * math.pi / points * product.astype(jnp.float32)
    cosine = jnp.cos(angles) / math.sqrt(points)
    sine_part = direction * jnp.sin(angles) / math.sqrt(points)
    matrix = jnp.stack([jnp.stack([cosine, sine_part], axis=1), jnp.stack([-sine_part, cosine], axis=1)], axis=0)
    matrix = matrix.astype(jnp.bfloat16)
    total_points = points * points
    twist_index = counter[:, None] * counter[None, :] % total_points
    twist_angle = 2.0 * math.pi / total_points * twist_index.astype(jnp.float32)
    return (matrix, jnp.cos(twist_angle), direction * jnp.sin(twist_angle))

def transform(values, tables):
    matrix, twist_real, twist_imag = tables
    points = matrix.shape[1]
    leading = values.shape[:-2]
    grid_values = values.reshape((-1, 2, points, points)).astype(jnp.float32)
    matrix_float = matrix.astype(jnp.float32)
    segmented = jnp.einsum('nrab,rasc->nbsc', grid_values, matrix_float, precision=lax.Precision.HIGHEST)
    real_part = segmented[:, :, 0, :]
    imag_part = segmented[:, :, 1, :]
    turned = jnp.stack([real_part * twist_real - imag_part * twist_imag, real_part * twist_imag + imag_part * twist_real], axis=2)
    turned = turned.astype(jnp.bfloat16).astype(jnp.float32)
    result = jnp.einsum('nbsc,sbtd->ntdc', turned, matrix_float, precision=lax.Precision.HIGHEST)
    return result.reshape(leading + (2, points * points))

def complex_times(first, second):
    real_part = first[..., 0, :] * second[..., 0, :] - first[..., 1, :] * second[..., 1, :]
    imag_part = first[..., 0, :] * second[..., 1, :] + first[..., 1, :] * second[..., 0, :]
    return jnp.stack([real_part, imag_part], axis=-2)

def conjugate(values):
    return jnp.stack([values[..., 0, :], -values[..., 1, :]], axis=-2)

def propagate(values, spectrum, forward, inverse):
    moved_on = transform(values.astype(jnp.bfloat16), forward)
    return transform(complex_times(moved_on, spectrum).astype(jnp.bfloat16), inverse)

def propagator(wave_nums, points_all):
    counter = jnp.arange(points_all, dtype=jnp.int32)
    folded = jnp.where(counter < points_all // 2, counter, counter - points_all).astype(jnp.float32)
    lateral = 2.0 * math.pi / points_all * folded
    excess = wave_nums[:, None] ** 2 - lateral[None, :] ** 2
    upward = jnp.sqrt(jnp.maximum(excess, 0.0)) * STEP_DEPTH
    damped = jnp.sqrt(jnp.maximum(-excess, 0.0)) * STEP_DEPTH
    real_part = jnp.where(excess > 0, jnp.cos(upward), jnp.exp(-damped))
    imag_part = jnp.where(excess > 0, jnp.sin(upward), jnp.zeros_like(upward))
    return jnp.stack([real_part, imag_part], axis=1)

def screens(wave_nums, slowness):
    phase = wave_nums[:, None, None] * STEP_DEPTH * slowness[None]
    return jnp.stack([jnp.cos(phase), jnp.sin(phase)], axis=2)

def encoded_sources(incident, encode, sources):
    shifts = jnp.arange(sources, dtype=jnp.int32)
    bit_set = encode[:, None] >> shifts[None, :] & 1
    signs_all = (1 - 2 * bit_set).astype(jnp.float32)
    return lax.optimization_barrier(jnp.sum(signs_all[:, :, None, None] * incident, axis=1))

def lookup_waves(freq_index, wavenum, table_size):
    onehot_rows = (freq_index[:, None] == jnp.arange(table_size, dtype=jnp.int32)[None, :]).astype(jnp.float32)
    return lax.optimization_barrier(jnp.sum(onehot_rows * wavenum[None, :], axis=1))

def reference(incident, encode, freq_index, wavenum, slowness, probes):
    points_all = SIDE * SIDE
    forward = dft_tables(SIDE, -1.0)
    inverse = dft_tables(SIDE, 1.0)
    sources = encoded_sources(incident, encode, NSRC)
    wave_nums = lookup_waves(freq_index, wavenum, NF)
    spectra = propagator(wave_nums, points_all)
    probe_float = probes.astype(jnp.float32)
    probe_planes = jnp.transpose(probe_float, (1, 0, 2))

    def one_group(totals, inputs):
        source, spectrum, wave_now = inputs
        plane_screens = screens(wave_now[None], slowness)[0]
        spectrum_row = spectrum[None]
        spectrum_back = conjugate(spectrum_row)

        def downward(carried, inputs_plane):
            background, tangent = carried
            screen_now, probe_now = inputs_plane
            background_next = complex_times(screen_now, propagate(background[None], spectrum_row, forward, inverse)[0])
            moved_on = complex_times(screen_now[None], propagate(tangent, spectrum_row, forward, inverse))
            scaled = wave_now * STEP_DEPTH * probe_now
            born_term = jnp.stack([-scaled * background_next[None, 1], scaled * background_next[None, 0]], axis=1)
            return ((background_next, moved_on + born_term), background_next)
        initial = (source, jnp.zeros((PROBES, 2, points_all), jnp.float32))
        (ending, tangent_end), backgrounds = lax.scan(downward, initial, (plane_screens, probe_planes))

        def upward(adjoint, inputs_plane):
            screen_now, background_next = inputs_plane
            correlation = wave_now * STEP_DEPTH * (background_next[None, 0] * adjoint[:, 1] - background_next[None, 1] * adjoint[:, 0])
            turned_back = complex_times(conjugate(screen_now)[None], adjoint)
            return (propagate(turned_back, spectrum_back, forward, inverse), correlation)
        unused_top, correlations = lax.scan(upward, tangent_end, (plane_screens, backgrounds), reverse=True)
        return (totals + correlations, None)
    totals, unused = lax.scan(one_group, jnp.zeros((PLANES, PROBES, points_all), jnp.float32), (sources, spectra, wave_nums))
    sketch = jnp.transpose(totals, (1, 0, 2)) / GROUPS + DAMPING * probe_float
    flattened = sketch.reshape(PROBES, PLANES * points_all)
    gram_matrix = jnp.dot(flattened, flattened.T, precision=lax.Precision.HIGHEST) / (PLANES * points_all)
    lower_factor = jnp.linalg.cholesky(gram_matrix)
    identity = jnp.eye(PROBES, dtype=jnp.float32)
    inverse_lower = lax.linalg.triangular_solve(lower_factor, identity, left_side=True, lower=True)
    sketch_basis = jnp.dot(inverse_lower, flattened, precision=lax.Precision.HIGHEST).reshape(PROBES, PLANES, points_all)
    return (sketch_basis, lower_factor.T)
```

```python
import math

import jax
import jax.numpy as jnp
from jax import lax
from jax.sharding import Mesh, PartitionSpec as P

SIDE = 64
CHIPS_Y = 8
CHIPS_Z = 8
CORES = 2
SRC_AXES = ("chip_y", "chip_z", "core")


DAMPING = 0.5
STEP_DEPTH = 1.0


def dft_tables(points, direction):
    counter = jnp.arange(points, dtype=jnp.int32)
    product = counter[:, None] * counter[None, :] % points
    angles = 2.0 * math.pi / points * product.astype(jnp.float32)
    cosine = jnp.cos(angles) / math.sqrt(points)
    sine_part = direction * jnp.sin(angles) / math.sqrt(points)
    matrix = jnp.stack(
        [jnp.stack([cosine, sine_part], axis=1), jnp.stack([-sine_part, cosine], axis=1)], axis=0
    )
    matrix = matrix.astype(jnp.bfloat16)
    total_points = points * points
    twist_index = counter[:, None] * counter[None, :] % total_points
    twist_angle = 2.0 * math.pi / total_points * twist_index.astype(jnp.float32)
    return (matrix, jnp.cos(twist_angle), direction * jnp.sin(twist_angle))


def transform(values, tables):
    matrix, twist_real, twist_imag = tables
    points = matrix.shape[1]
    leading = values.shape[:-2]
    grid_values = values.reshape((-1, 2 * points, points))
    square = matrix.reshape(2 * points, 2 * points)
    segmented = jnp.einsum("nkb,km->nbm", grid_values, square, preferred_element_type=jnp.float32)
    real_part = segmented[:, :, :points]
    imag_part = segmented[:, :, points:]
    turned = jnp.concatenate(
        [
            real_part * twist_real - imag_part * twist_imag,
            real_part * twist_imag + imag_part * twist_real,
        ],
        axis=-1,
    )
    turned = turned.astype(jnp.bfloat16).reshape((-1, points, 2, points))
    result = jnp.einsum("nbsc,sbtd->ntdc", turned, matrix, preferred_element_type=jnp.float32)
    return result.reshape(leading + (2, points * points))


def complex_times(first, second):
    real_part = first[..., 0, :] * second[..., 0, :] - first[..., 1, :] * second[..., 1, :]
    imag_part = first[..., 0, :] * second[..., 1, :] + first[..., 1, :] * second[..., 0, :]
    return jnp.stack([real_part, imag_part], axis=-2)


def conjugate(values):
    return jnp.stack([values[..., 0, :], -values[..., 1, :]], axis=-2)


def propagate(values, spectrum, forward, inverse):
    moved_on = transform(values.astype(jnp.bfloat16), forward)
    return transform(complex_times(moved_on, spectrum).astype(jnp.bfloat16), inverse)


def propagator(wave_nums, points_all):
    counter = jnp.arange(points_all, dtype=jnp.int32)
    folded = jnp.where(counter < points_all // 2, counter, counter - points_all).astype(jnp.float32)
    lateral = 2.0 * math.pi / points_all * folded
    excess = wave_nums[:, None] ** 2 - lateral[None, :] ** 2
    upward = jnp.sqrt(jnp.maximum(excess, 0.0)) * STEP_DEPTH
    damped = jnp.sqrt(jnp.maximum(-excess, 0.0)) * STEP_DEPTH
    real_part = jnp.where(excess > 0, jnp.cos(upward), jnp.exp(-damped))
    imag_part = jnp.where(excess > 0, jnp.sin(upward), jnp.zeros_like(upward))
    return jnp.stack([real_part, imag_part], axis=1)


def screens(wave_nums, slowness):
    phase = wave_nums[:, None, None] * STEP_DEPTH * slowness[None]
    return jnp.stack([jnp.cos(phase), jnp.sin(phase)], axis=2)


def encoded_sources(incident, encode, sources):
    shifts = jnp.arange(sources, dtype=jnp.int32)
    bit_set = encode[:, None] >> shifts[None, :] & 1
    signs_all = (1 - 2 * bit_set).astype(jnp.float32)
    return jnp.sum(signs_all[:, :, None, None] * incident, axis=1)


def lookup_waves(freq_index, wavenum, table_size):
    onehot_rows = (freq_index[:, None] == jnp.arange(table_size, dtype=jnp.int32)[None, :]).astype(
        jnp.float32
    )
    return jnp.sum(onehot_rows * wavenum[None, :], axis=1)


def shards(incident, encode, freq_index, wavenum, slowness, probes):
    points_all = SIDE * SIDE
    forward = dft_tables(SIDE, -1.0)
    inverse = dft_tables(SIDE, 1.0)
    group_count = incident.shape[0]
    probe_count = probes.shape[0]
    src_count = lax.axis_size(SRC_AXES)
    depth_count = lax.axis_size("depth")
    slowness_all = lax.all_gather(slowness, "depth", axis=0, tiled=True)
    plane_count = slowness_all.shape[0]
    probe_mine = lax.all_to_all(probes, "depth", 0, 1, tiled=True).astype(jnp.float32)
    sources = encoded_sources(incident, encode, incident.shape[1])
    wave_nums = lookup_waves(freq_index, wavenum, wavenum.shape[0])
    spectra = propagator(wave_nums, points_all)
    spectra_back = conjugate(spectra)
    plane_screens = screens(wave_nums, slowness_all)
    born_scale = wave_nums * STEP_DEPTH

    fields = []
    current = sources
    for plane in range(plane_count):
        current = complex_times(plane_screens[:, plane], propagate(current, spectra, forward, inverse))
        fields.append(current)

    def born(plane):
        scaled = born_scale[:, None, None] * probe_mine[None, :, plane]
        background = fields[plane]
        return jnp.stack([-scaled * background[:, None, 1], scaled * background[:, None, 0]], axis=2)

    tangent = born(0)
    for plane in range(1, plane_count):
        moved_on = complex_times(
            plane_screens[:, plane][:, None], propagate(tangent, spectra[:, None], forward, inverse)
        )
        tangent = moved_on + born(plane)

    adjoint = tangent
    pieces = [None] * plane_count
    for plane in reversed(range(plane_count)):
        background = fields[plane]
        product_terms = born_scale[:, None, None] * (
            background[:, None, 0] * adjoint[:, :, 1] - background[:, None, 1] * adjoint[:, :, 0]
        )
        pieces[plane] = jnp.sum(product_terms, axis=0)
        if plane > 0:
            turned_back = complex_times(conjugate(plane_screens[:, plane])[:, None], adjoint)
            adjoint = propagate(turned_back, spectra_back[:, None], forward, inverse)
    sketch_part = jnp.stack(pieces, axis=1)
    rows, planes = sketch_part.shape[0], sketch_part.shape[1]
    by_axes = sketch_part.reshape(rows, planes, CHIPS_Y, CHIPS_Z, CORES, -1)
    by_axes = jnp.transpose(by_axes, (4, 3, 2, 0, 1, 5))
    summed = lax.psum_scatter(by_axes, "core", scatter_dimension=0)
    summed = lax.psum_scatter(summed, "chip_z", scatter_dimension=0)
    summed = lax.psum_scatter(summed, "chip_y", scatter_dimension=0)
    summed = lax.all_gather(summed, "depth", axis=0, tiled=True)
    slab_width = summed.shape[2]
    src_index = lax.axis_index(SRC_AXES)
    local_probes = lax.dynamic_slice_in_dim(probes, src_index * slab_width, slab_width, 2)
    local_probes = lax.all_gather(local_probes, "depth", axis=1, tiled=True).astype(jnp.float32)
    sketch_all = summed / (group_count * src_count) + DAMPING * local_probes
    flattened_all = sketch_all.reshape(probe_count, -1)
    row_total = flattened_all.shape[1] * src_count
    gram_local = jnp.dot(flattened_all, flattened_all.T, precision=lax.Precision.HIGHEST) / row_total
    gram_matrix = lax.psum(gram_local, "core")
    gram_matrix = lax.psum(gram_matrix, "chip_z")
    gram_matrix = lax.psum(gram_matrix, "chip_y")
    sketch = lax.dynamic_slice_in_dim(sketch_all, lax.axis_index("depth"), 1, 1)
    local_planes = 1
    flattened = sketch.reshape(probe_count, local_planes * slab_width)
    lower_factor = jnp.linalg.cholesky(gram_matrix)
    identity = jnp.eye(probe_count, dtype=jnp.float32)
    inverse_lower = lax.linalg.triangular_solve(lower_factor, identity, left_side=True, lower=True)
    sketch_basis = jnp.dot(inverse_lower, flattened, precision=lax.Precision.HIGHEST).reshape(
        probe_count, local_planes, slab_width
    )
    return (sketch_basis, lower_factor.T)


def solution(mesh):
    src_size, depth_size = mesh.devices.shape
    cut = mesh.devices.reshape(CHIPS_Y, CHIPS_Z, CORES, depth_size)
    fine = Mesh(cut, SRC_AXES + ("depth",))
    in_specs = (
        P(SRC_AXES, None, None, None),
        P(SRC_AXES),
        P(SRC_AXES),
        P(),
        P("depth", None),
        P(None, "depth", None),
    )
    out_specs = (P(None, "depth", SRC_AXES), P())
    return jax.shard_map(shards, mesh=fine, in_specs=in_specs, out_specs=out_specs, check_vma=False)
```

```python
import math

import jax
import jax.numpy as jnp
from jax import lax
from jax.experimental import pallas as pl
from jax.experimental.pallas import tpu as pltpu
from jax.sharding import Mesh, PartitionSpec as P

SIDE = 64
CHIPS_Y = 8
CHIPS_Z = 8
CORES = 2
SRC_AXES = ("chip_y", "chip_z", "core")


DAMPING = 0.5
STEP_DEPTH = 1.0


def dft_tables(points, direction):
    counter = jnp.arange(points, dtype=jnp.int32)
    product = counter[:, None] * counter[None, :] % points
    angles = 2.0 * math.pi / points * product.astype(jnp.float32)
    cosine = jnp.cos(angles) / math.sqrt(points)
    sine_part = direction * jnp.sin(angles) / math.sqrt(points)
    matrix = jnp.stack(
        [jnp.stack([cosine, sine_part], axis=1), jnp.stack([-sine_part, cosine], axis=1)], axis=0
    )
    matrix = matrix.astype(jnp.bfloat16)
    total_points = points * points
    twist_index = counter[:, None] * counter[None, :] % total_points
    twist_angle = 2.0 * math.pi / total_points * twist_index.astype(jnp.float32)
    return (matrix, jnp.cos(twist_angle), direction * jnp.sin(twist_angle))


def transform(values, tables):
    matrix, twist_real, twist_imag = tables
    points = matrix.shape[1]
    leading = values.shape[:-2]
    grid_values = values.reshape((-1, 2 * points, points))
    square = matrix.reshape(2 * points, 2 * points)
    segmented = jnp.einsum("nkb,km->nbm", grid_values, square, preferred_element_type=jnp.float32)
    real_part = segmented[:, :, :points]
    imag_part = segmented[:, :, points:]
    turned = jnp.concatenate(
        [
            real_part * twist_real - imag_part * twist_imag,
            real_part * twist_imag + imag_part * twist_real,
        ],
        axis=-1,
    )
    turned = turned.astype(jnp.bfloat16).reshape((-1, points, 2, points))
    result = jnp.einsum("nbsc,sbtd->ntdc", turned, matrix, preferred_element_type=jnp.float32)
    return result.reshape(leading + (2, points * points))


def complex_times(first, second):
    real_part = first[..., 0, :] * second[..., 0, :] - first[..., 1, :] * second[..., 1, :]
    imag_part = first[..., 0, :] * second[..., 1, :] + first[..., 1, :] * second[..., 0, :]
    return jnp.stack([real_part, imag_part], axis=-2)


def conjugate(values):
    return jnp.stack([values[..., 0, :], -values[..., 1, :]], axis=-2)


def propagate(values, spectrum, forward, inverse):
    moved_on = transform(values.astype(jnp.bfloat16), forward)
    return transform(complex_times(moved_on, spectrum).astype(jnp.bfloat16), inverse)


def propagator(wave_nums, points_all):
    counter = jnp.arange(points_all, dtype=jnp.int32)
    folded = jnp.where(counter < points_all // 2, counter, counter - points_all).astype(jnp.float32)
    lateral = 2.0 * math.pi / points_all * folded
    excess = wave_nums[:, None] ** 2 - lateral[None, :] ** 2
    upward = jnp.sqrt(jnp.maximum(excess, 0.0)) * STEP_DEPTH
    damped = jnp.sqrt(jnp.maximum(-excess, 0.0)) * STEP_DEPTH
    real_part = jnp.where(excess > 0, jnp.cos(upward), jnp.exp(-damped))
    imag_part = jnp.where(excess > 0, jnp.sin(upward), jnp.zeros_like(upward))
    return jnp.stack([real_part, imag_part], axis=1)


def screens(wave_nums, slowness):
    phase = wave_nums[:, None, None] * STEP_DEPTH * slowness[None]
    return jnp.stack([jnp.cos(phase), jnp.sin(phase)], axis=2)


def encoded_sources(incident, encode, sources):
    shifts = jnp.arange(sources, dtype=jnp.int32)
    bit_set = encode[:, None] >> shifts[None, :] & 1
    signs_all = (1 - 2 * bit_set).astype(jnp.float32)
    return jnp.sum(signs_all[:, :, None, None] * incident, axis=1)


def lookup_waves(freq_index, wavenum, table_size):
    onehot_rows = (freq_index[:, None] == jnp.arange(table_size, dtype=jnp.int32)[None, :]).astype(
        jnp.float32
    )
    return jnp.sum(onehot_rows * wavenum[None, :], axis=1)


def gram_sum_kernel(stages, part_ref, out_ref, *scratch):
    count = len(stages)
    slots = scratch[:count]
    send_sems, recv_sems, carried = scratch[count], scratch[count + 1], scratch[count + 2]
    barrier = pltpu.get_barrier_semaphore()
    peers_total = 0
    for axis, size in stages:
        me = lax.axis_index(axis)
        for step in range(1, size):
            pl.semaphore_signal(barrier, inc=1, device_id={axis: lax.rem(me + step, size)},
                                device_id_type=pl.DeviceIdType.MESH)
            peers_total += 1
    pl.semaphore_wait(barrier, peers_total)
    carried[...] = part_ref[...]
    used = 0
    offset = 0
    for stage, (axis, size) in enumerate(stages):
        me = lax.axis_index(axis)
        slot = slots[stage]
        copies = []
        for step in range(1, size):
            copy = pltpu.make_async_remote_copy(
                src_ref=carried,
                dst_ref=slot.at[me],
                send_sem=send_sems.at[used + step - 1],
                recv_sem=recv_sems.at[offset + me],
                device_id={axis: lax.rem(me + step, size)},
                device_id_type=pl.DeviceIdType.MESH,
            )
            copy.start()
            copies.append(copy)
        slot[me] = carried[...]
        for copy in copies:
            copy.wait_send()
        for step in range(1, size):
            sender = lax.rem(me + size - step, size)
            incoming = pltpu.make_async_remote_copy(
                src_ref=carried,
                dst_ref=slot.at[sender],
                send_sem=send_sems.at[used + step - 1],
                recv_sem=recv_sems.at[offset + sender],
                device_id={axis: lax.rem(me + step, size)},
                device_id_type=pl.DeviceIdType.MESH,
            )
            incoming.wait_recv()
        used += size - 1
        offset += size
        total = slot[0]
        for member in range(1, size):
            total = total + slot[member]
        carried[...] = total
    out_ref[...] = carried[...]


def gram_sum(part, stages):
    stages = [(axis, size) for axis, size in stages if size > 1]
    sends = sum(size - 1 for _, size in stages)
    scratch = [pltpu.VMEM((size,) + part.shape, jnp.float32) for _, size in stages]
    scratch += [
        pltpu.SemaphoreType.DMA((max(sends, 1),)),
        pltpu.SemaphoreType.DMA((max(sum(size for _, size in stages), 1),)),
        pltpu.VMEM(part.shape, jnp.float32),
    ]
    return pl.pallas_call(
        lambda *refs: gram_sum_kernel(stages, *refs),
        out_shape=jax.ShapeDtypeStruct(part.shape, jnp.float32),
        in_specs=[pl.BlockSpec(memory_space=pltpu.VMEM)],
        out_specs=pl.BlockSpec(memory_space=pltpu.VMEM),
        scratch_shapes=scratch,
        compiler_params=pltpu.CompilerParams(collective_id=0, has_side_effects=True),
    )(part)


def shards(incident, encode, freq_index, wavenum, slowness, probes):
    points_all = SIDE * SIDE
    forward = dft_tables(SIDE, -1.0)
    inverse = dft_tables(SIDE, 1.0)
    group_count = incident.shape[0]
    probe_count = probes.shape[0]
    src_count = lax.axis_size(SRC_AXES)
    depth_count = lax.axis_size("depth")
    spread = jnp.broadcast_to(slowness[None], (depth_count,) + slowness.shape)
    slowness_all = lax.all_to_all(spread, "depth", 0, 0, tiled=True).reshape(-1, slowness.shape[-1])
    plane_count = slowness_all.shape[0]
    probe_mine = lax.all_to_all(probes, "depth", 0, 1, tiled=True).astype(jnp.float32)
    sources = encoded_sources(incident, encode, incident.shape[1])
    wave_nums = lookup_waves(freq_index, wavenum, wavenum.shape[0])
    spectra = propagator(wave_nums, points_all)
    spectra_back = conjugate(spectra)
    plane_screens = screens(wave_nums, slowness_all)
    born_scale = wave_nums * STEP_DEPTH

    fields = []
    current = sources
    for plane in range(plane_count):
        current = complex_times(plane_screens[:, plane], propagate(current, spectra, forward, inverse))
        fields.append(current)

    def born(plane):
        scaled = born_scale[:, None, None] * probe_mine[None, :, plane]
        background = fields[plane]
        return jnp.stack([-scaled * background[:, None, 1], scaled * background[:, None, 0]], axis=2)

    tangent = born(0)
    for plane in range(1, plane_count):
        moved_on = complex_times(
            plane_screens[:, plane][:, None], propagate(tangent, spectra[:, None], forward, inverse)
        )
        tangent = moved_on + born(plane)

    adjoint = tangent
    pieces = [None] * plane_count
    for plane in reversed(range(plane_count)):
        background = fields[plane]
        product_terms = born_scale[:, None, None] * (
            background[:, None, 0] * adjoint[:, :, 1] - background[:, None, 1] * adjoint[:, :, 0]
        )
        pieces[plane] = jnp.sum(product_terms, axis=0)
        if plane > 0:
            turned_back = complex_times(conjugate(plane_screens[:, plane])[:, None], adjoint)
            adjoint = propagate(turned_back, spectra_back[:, None], forward, inverse)
    sketch_part = jnp.stack(pieces, axis=1)
    rows, planes = sketch_part.shape[0], sketch_part.shape[1]
    by_axes = sketch_part.reshape(rows, planes, CHIPS_Y, CHIPS_Z, CORES, -1)
    by_axes = jnp.transpose(by_axes, (4, 3, 2, 0, 1, 5))
    summed = lax.psum_scatter(by_axes, "core", scatter_dimension=0)
    summed = lax.psum_scatter(summed, "chip_z", scatter_dimension=0)
    summed = lax.psum_scatter(summed, "chip_y", scatter_dimension=0)
    slab_width = summed.shape[-1]
    src_index = lax.axis_index(SRC_AXES)
    probe_slab = lax.dynamic_slice_in_dim(probes, src_index * slab_width, slab_width, 2)
    probe_slab = jnp.transpose(probe_slab.reshape(depth_count, rows, slab_width), (1, 0, 2))
    both = jnp.stack([summed.reshape(rows, planes, slab_width), probe_slab.astype(jnp.float32)])
    both = lax.all_gather(both, "depth", axis=0)
    summed = both[:, 0].reshape(probe_count, planes, slab_width)
    local_probes = jnp.transpose(both[:, 1], (2, 1, 0, 3)).reshape(probe_count, planes, slab_width)
    sketch_all = summed / (group_count * src_count) + DAMPING * local_probes
    flattened_all = sketch_all.reshape(probe_count, -1)
    row_total = flattened_all.shape[1] * src_count
    gram_local = jnp.dot(flattened_all, flattened_all.T, precision=lax.Precision.HIGHEST) / row_total
    stage_sizes = [(axis, lax.axis_size(axis)) for axis in ("core", "chip_z", "chip_y")]
    gram_matrix = gram_sum(gram_local, stage_sizes)
    sketch = lax.dynamic_slice_in_dim(sketch_all, lax.axis_index("depth"), 1, 1)
    local_planes = 1
    flattened = sketch.reshape(probe_count, local_planes * slab_width)
    lower_factor = jnp.linalg.cholesky(gram_matrix)
    identity = jnp.eye(probe_count, dtype=jnp.float32)
    inverse_lower = lax.linalg.triangular_solve(lower_factor, identity, left_side=True, lower=True)
    sketch_basis = jnp.dot(inverse_lower, flattened, precision=lax.Precision.HIGHEST).reshape(
        probe_count, local_planes, slab_width
    )
    return (sketch_basis, lower_factor.T)


def solution(mesh):
    src_size, depth_size = mesh.devices.shape
    cut = mesh.devices.reshape(CHIPS_Y, CHIPS_Z, CORES, depth_size)
    fine = Mesh(cut, SRC_AXES + ("depth",))
    in_specs = (
        P(SRC_AXES, None, None, None),
        P(SRC_AXES),
        P(SRC_AXES),
        P(),
        P("depth", None),
        P(None, "depth", None),
    )
    out_specs = (P(None, "depth", SRC_AXES), P())
    return jax.shard_map(shards, mesh=fine, in_specs=in_specs, out_specs=out_specs, check_vma=False)
```

```python
import math

import jax
import jax.numpy as jnp
from jax import lax
from jax.experimental import pallas as pl
from jax.experimental.pallas import tpu as pltpu
from jax.sharding import Mesh, PartitionSpec as P

SIDE = 64
CHIPS_Y = 8
CHIPS_Z = 8
CORES = 2
SRC_AXES = ("chip_y", "chip_z", "core")


DAMPING = 0.5
STEP_DEPTH = 1.0


def dft_tables(points, direction):
    counter = jnp.arange(points, dtype=jnp.int32)
    product = counter[:, None] * counter[None, :] % points
    angles = 2.0 * math.pi / points * product.astype(jnp.float32)
    cosine = jnp.cos(angles) / math.sqrt(points)
    sine_part = direction * jnp.sin(angles) / math.sqrt(points)
    matrix = jnp.stack(
        [jnp.stack([cosine, sine_part], axis=1), jnp.stack([-sine_part, cosine], axis=1)], axis=0
    )
    matrix = matrix.astype(jnp.bfloat16)
    total_points = points * points
    twist_index = counter[:, None] * counter[None, :] % total_points
    twist_angle = 2.0 * math.pi / total_points * twist_index.astype(jnp.float32)
    return (matrix, jnp.cos(twist_angle), direction * jnp.sin(twist_angle))


def transform(values, tables):
    matrix, twist_real, twist_imag = tables
    points = matrix.shape[1]
    leading = values.shape[:-2]
    grid_values = values.reshape((-1, 2 * points, points))
    square = matrix.reshape(2 * points, 2 * points)
    segmented = jnp.einsum("nkb,km->nbm", grid_values, square, preferred_element_type=jnp.float32)
    real_part = segmented[:, :, :points]
    imag_part = segmented[:, :, points:]
    turned = jnp.concatenate(
        [
            real_part * twist_real - imag_part * twist_imag,
            real_part * twist_imag + imag_part * twist_real,
        ],
        axis=-1,
    )
    turned = turned.astype(jnp.bfloat16).reshape((-1, points, 2, points))
    result = jnp.einsum("nbsc,sbtd->ntdc", turned, matrix, preferred_element_type=jnp.float32)
    return result.reshape(leading + (2, points * points))


def complex_times(first, second):
    real_part = first[..., 0, :] * second[..., 0, :] - first[..., 1, :] * second[..., 1, :]
    imag_part = first[..., 0, :] * second[..., 1, :] + first[..., 1, :] * second[..., 0, :]
    return jnp.stack([real_part, imag_part], axis=-2)


def conjugate(values):
    return jnp.stack([values[..., 0, :], -values[..., 1, :]], axis=-2)


def propagate(values, spectrum, forward, inverse):
    moved_on = transform(values.astype(jnp.bfloat16), forward)
    return transform(complex_times(moved_on, spectrum).astype(jnp.bfloat16), inverse)


def propagator(wave_nums, points_all):
    counter = jnp.arange(points_all, dtype=jnp.int32)
    folded = jnp.where(counter < points_all // 2, counter, counter - points_all).astype(jnp.float32)
    lateral = 2.0 * math.pi / points_all * folded
    excess = wave_nums[:, None] ** 2 - lateral[None, :] ** 2
    upward = jnp.sqrt(jnp.maximum(excess, 0.0)) * STEP_DEPTH
    damped = jnp.sqrt(jnp.maximum(-excess, 0.0)) * STEP_DEPTH
    real_part = jnp.where(excess > 0, jnp.cos(upward), jnp.exp(-damped))
    imag_part = jnp.where(excess > 0, jnp.sin(upward), jnp.zeros_like(upward))
    return jnp.stack([real_part, imag_part], axis=1)


def screens(wave_nums, slowness):
    phase = wave_nums[:, None, None] * STEP_DEPTH * slowness[None]
    return jnp.stack([jnp.cos(phase), jnp.sin(phase)], axis=2)


def encoded_sources(incident, encode, sources):
    shifts = jnp.arange(sources, dtype=jnp.int32)
    bit_set = encode[:, None] >> shifts[None, :] & 1
    signs_all = (1 - 2 * bit_set).astype(jnp.float32)
    return jnp.sum(signs_all[:, :, None, None] * incident, axis=1)


def lookup_waves(freq_index, wavenum, table_size):
    onehot_rows = (freq_index[:, None] == jnp.arange(table_size, dtype=jnp.int32)[None, :]).astype(
        jnp.float32
    )
    return jnp.sum(onehot_rows * wavenum[None, :], axis=1)


def gram_sum_kernel(stages, part_ref, out_ref, *scratch):
    count = len(stages)
    slots = scratch[:count]
    send_sems, recv_sems, carried = scratch[count], scratch[count + 1], scratch[count + 2]
    barrier = pltpu.get_barrier_semaphore()
    peers_total = 0
    for axis, size in stages:
        me = lax.axis_index(axis)
        for step in range(1, size):
            pl.semaphore_signal(barrier, inc=1, device_id={axis: lax.rem(me + step, size)},
                                device_id_type=pl.DeviceIdType.MESH)
            peers_total += 1
    pl.semaphore_wait(barrier, peers_total)
    carried[...] = part_ref[...]
    used = 0
    offset = 0
    for stage, (axis, size) in enumerate(stages):
        me = lax.axis_index(axis)
        slot = slots[stage]
        copies = []
        for step in range(1, size):
            copy = pltpu.make_async_remote_copy(
                src_ref=carried,
                dst_ref=slot.at[me],
                send_sem=send_sems.at[used + step - 1],
                recv_sem=recv_sems.at[offset + me],
                device_id={axis: lax.rem(me + step, size)},
                device_id_type=pl.DeviceIdType.MESH,
            )
            copy.start()
            copies.append(copy)
        slot[me] = carried[...]
        for copy in copies:
            copy.wait_send()
        for step in range(1, size):
            sender = lax.rem(me + size - step, size)
            incoming = pltpu.make_async_remote_copy(
                src_ref=carried,
                dst_ref=slot.at[sender],
                send_sem=send_sems.at[used + step - 1],
                recv_sem=recv_sems.at[offset + sender],
                device_id={axis: lax.rem(me + step, size)},
                device_id_type=pl.DeviceIdType.MESH,
            )
            incoming.wait_recv()
        used += size - 1
        offset += size
        total = slot[0]
        for member in range(1, size):
            total = total + slot[member]
        carried[...] = total
    out_ref[...] = carried[...]


def gram_sum(part, stages):
    stages = [(axis, size) for axis, size in stages if size > 1]
    sends = sum(size - 1 for _, size in stages)
    scratch = [pltpu.VMEM((size,) + part.shape, jnp.float32) for _, size in stages]
    scratch += [
        pltpu.SemaphoreType.DMA((max(sends, 1),)),
        pltpu.SemaphoreType.DMA((max(sum(size for _, size in stages), 1),)),
        pltpu.VMEM(part.shape, jnp.float32),
    ]
    return pl.pallas_call(
        lambda *refs: gram_sum_kernel(stages, *refs),
        out_shape=jax.ShapeDtypeStruct(part.shape, jnp.float32),
        in_specs=[pl.BlockSpec(memory_space=pltpu.VMEM)],
        out_specs=pl.BlockSpec(memory_space=pltpu.VMEM),
        scratch_shapes=scratch,
        compiler_params=pltpu.CompilerParams(collective_id=0, has_side_effects=True),
    )(part)


def exchange(axis, size, current, slot, send_sems, recv_sems, offset, whole=False):
    me = lax.axis_index(axis)
    copies = []
    for step in range(1, size):
        peer = lax.rem(me + step, size)
        copy = pltpu.make_async_remote_copy(
            src_ref=current if whole else current.at[peer],
            dst_ref=slot.at[me],
            send_sem=send_sems.at[offset + peer],
            recv_sem=recv_sems.at[offset + me],
            device_id={axis: peer},
            device_id_type=pl.DeviceIdType.MESH,
        )
        copy.start()
        copies.append(copy)
    for copy in copies:
        copy.wait_send()
    for step in range(1, size):
        sender = lax.rem(me + size - step, size)
        incoming = pltpu.make_async_remote_copy(
            src_ref=current if whole else current.at[sender],
            dst_ref=slot.at[sender],
            send_sem=send_sems.at[offset + sender],
            recv_sem=recv_sems.at[offset + sender],
            device_id={axis: sender},
            device_id_type=pl.DeviceIdType.MESH,
        )
        incoming.wait_recv()
    return me


def scatter_kernel(stages, part_ref, extra_ref, out_ref, *scratch):
    count = len(stages)
    slots = scratch[:count]
    sums = scratch[count : 2 * count - 1]
    mine, gathered, send_sems, recv_sems = scratch[2 * count - 1 :]
    barrier = pltpu.get_barrier_semaphore()
    peers_total = 0
    for axis, size in stages + [("depth", out_ref.shape[0])]:
        me = lax.axis_index(axis)
        for step in range(1, size):
            pl.semaphore_signal(barrier, inc=1, device_id={axis: lax.rem(me + step, size)},
                                device_id_type=pl.DeviceIdType.MESH)
            peers_total += 1
    pl.semaphore_wait(barrier, peers_total)
    current = part_ref
    offset = 0
    for stage, (axis, size) in enumerate(stages):
        me = exchange(axis, size, current, slots[stage], send_sems, recv_sems, offset)
        offset += size
        total = current[me]
        for step in range(1, size):
            total = total + slots[stage][lax.rem(me + size - step, size)]
        if stage + 1 < count:
            sums[stage][...] = total
            current = sums[stage]
        else:
            mine[0] = total
    mine[1] = extra_ref[...]
    depth_size = out_ref.shape[0]
    me = exchange("depth", depth_size, mine, gathered, send_sems, recv_sems, offset, whole=True)
    gathered[me] = mine[...]
    out_ref[...] = gathered[...]


def scatter_gather(part, extra, stages, depth_size):
    stages = [(axis, size) for axis, size in stages if size > 1]
    part = part.reshape(tuple(size for _, size in stages) + part.shape[-2:])
    scratch = [pltpu.VMEM(part.shape[stage:], jnp.float32) for stage in range(len(stages))]
    scratch += [pltpu.VMEM(part.shape[stage + 1 :], jnp.float32) for stage in range(len(stages) - 1)]
    block = (2,) + extra.shape
    scratch += [
        pltpu.VMEM(block, jnp.float32),
        pltpu.VMEM((depth_size,) + block, jnp.float32),
        pltpu.SemaphoreType.DMA((sum(size for _, size in stages) + depth_size,)),
        pltpu.SemaphoreType.DMA((sum(size for _, size in stages) + depth_size,)),
    ]
    return pl.pallas_call(
        lambda *refs: scatter_kernel(stages, *refs),
        out_shape=jax.ShapeDtypeStruct((depth_size,) + block, jnp.float32),
        in_specs=[pl.BlockSpec(memory_space=pltpu.VMEM)] * 2,
        out_specs=pl.BlockSpec(memory_space=pltpu.VMEM),
        scratch_shapes=scratch,
        compiler_params=pltpu.CompilerParams(collective_id=1, has_side_effects=True),
    )(part, extra)


def shards(incident, encode, freq_index, wavenum, slowness, probes):
    points_all = SIDE * SIDE
    forward = dft_tables(SIDE, -1.0)
    inverse = dft_tables(SIDE, 1.0)
    group_count = incident.shape[0]
    probe_count = probes.shape[0]
    src_count = lax.axis_size(SRC_AXES)
    depth_count = lax.axis_size("depth")
    spread = jnp.broadcast_to(slowness[None], (depth_count,) + slowness.shape)
    slowness_all = lax.all_to_all(spread, "depth", 0, 0, tiled=True).reshape(-1, slowness.shape[-1])
    plane_count = slowness_all.shape[0]
    probe_mine = lax.all_to_all(probes, "depth", 0, 1, tiled=True).astype(jnp.float32)
    sources = encoded_sources(incident, encode, incident.shape[1])
    wave_nums = lookup_waves(freq_index, wavenum, wavenum.shape[0])
    spectra = propagator(wave_nums, points_all)
    spectra_back = conjugate(spectra)
    plane_screens = screens(wave_nums, slowness_all)
    born_scale = wave_nums * STEP_DEPTH

    fields = []
    current = sources
    for plane in range(plane_count):
        current = complex_times(plane_screens[:, plane], propagate(current, spectra, forward, inverse))
        fields.append(current)

    def born(plane):
        scaled = born_scale[:, None, None] * probe_mine[None, :, plane]
        background = fields[plane]
        return jnp.stack([-scaled * background[:, None, 1], scaled * background[:, None, 0]], axis=2)

    tangent = born(0)
    for plane in range(1, plane_count):
        moved_on = complex_times(
            plane_screens[:, plane][:, None], propagate(tangent, spectra[:, None], forward, inverse)
        )
        tangent = moved_on + born(plane)

    adjoint = tangent
    pieces = [None] * plane_count
    for plane in reversed(range(plane_count)):
        background = fields[plane]
        product_terms = born_scale[:, None, None] * (
            background[:, None, 0] * adjoint[:, :, 1] - background[:, None, 1] * adjoint[:, :, 0]
        )
        pieces[plane] = jnp.sum(product_terms, axis=0)
        if plane > 0:
            turned_back = complex_times(conjugate(plane_screens[:, plane])[:, None], adjoint)
            adjoint = propagate(turned_back, spectra_back[:, None], forward, inverse)
    sketch_part = jnp.stack(pieces, axis=1)
    rows, planes = sketch_part.shape[0], sketch_part.shape[1]
    by_axes = sketch_part.reshape(rows, planes, CHIPS_Y, CHIPS_Z, CORES, -1)
    slab_width = by_axes.shape[-1]
    by_axes = jnp.transpose(by_axes, (4, 3, 2, 0, 1, 5)).reshape(
        CORES, CHIPS_Z, CHIPS_Y, rows, planes * slab_width
    )
    src_index = lax.axis_index(SRC_AXES)
    probe_slab = lax.dynamic_slice_in_dim(probes, src_index * slab_width, slab_width, 2)
    probe_slab = jnp.transpose(probe_slab.reshape(depth_count, rows, slab_width), (1, 0, 2))
    probe_slab = probe_slab.reshape(rows, depth_count * slab_width).astype(jnp.float32)
    stage_sizes = [("core", CORES), ("chip_z", CHIPS_Z), ("chip_y", CHIPS_Y)]
    both = scatter_gather(by_axes, probe_slab, stage_sizes, depth_count)
    summed = both[:, 0].reshape(probe_count, planes, slab_width)
    local_probes = jnp.transpose(
        both[:, 1].reshape(depth_count, rows, depth_count, slab_width), (2, 1, 0, 3)
    ).reshape(probe_count, planes, slab_width)
    sketch_all = summed / (group_count * src_count) + DAMPING * local_probes
    flattened_all = sketch_all.reshape(probe_count, -1)
    row_total = flattened_all.shape[1] * src_count
    gram_local = jnp.dot(flattened_all, flattened_all.T, precision=lax.Precision.HIGHEST) / row_total
    stage_sizes = [(axis, lax.axis_size(axis)) for axis in ("core", "chip_z", "chip_y")]
    gram_matrix = gram_sum(gram_local, stage_sizes)
    sketch = lax.dynamic_slice_in_dim(sketch_all, lax.axis_index("depth"), 1, 1)
    local_planes = 1
    flattened = sketch.reshape(probe_count, local_planes * slab_width)
    lower_factor = jnp.linalg.cholesky(gram_matrix)
    identity = jnp.eye(probe_count, dtype=jnp.float32)
    inverse_lower = lax.linalg.triangular_solve(lower_factor, identity, left_side=True, lower=True)
    sketch_basis = jnp.dot(inverse_lower, flattened, precision=lax.Precision.HIGHEST).reshape(
        probe_count, local_planes, slab_width
    )
    return (sketch_basis, lower_factor.T)


def solution(mesh):
    src_size, depth_size = mesh.devices.shape
    cut = mesh.devices.reshape(CHIPS_Y, CHIPS_Z, CORES, depth_size)
    fine = Mesh(cut, SRC_AXES + ("depth",))
    in_specs = (
        P(SRC_AXES, None, None, None),
        P(SRC_AXES),
        P(SRC_AXES),
        P(),
        P("depth", None),
        P(None, "depth", None),
    )
    out_specs = (P(None, "depth", SRC_AXES), P())
    return jax.shard_map(shards, mesh=fine, in_specs=in_specs, out_specs=out_specs, check_vma=False)
```

```python
import math

import jax
import jax.numpy as jnp
from jax import lax
from jax.experimental import pallas as pl
from jax.experimental.pallas import tpu as pltpu
from jax.sharding import Mesh, PartitionSpec as P

SIDE = 64
CHIPS_Y = 8
CHIPS_Z = 8
CORES = 2
SRC_AXES = ("chip_y", "chip_z", "core")


DAMPING = 0.5
STEP_DEPTH = 1.0


def dft_tables(points, direction):
    counter = jnp.arange(points, dtype=jnp.int32)
    product = counter[:, None] * counter[None, :] % points
    angles = 2.0 * math.pi / points * product.astype(jnp.float32)
    cosine = jnp.cos(angles) / math.sqrt(points)
    sine_part = direction * jnp.sin(angles) / math.sqrt(points)
    matrix = jnp.stack(
        [jnp.stack([cosine, sine_part], axis=1), jnp.stack([-sine_part, cosine], axis=1)], axis=0
    )
    matrix = matrix.astype(jnp.bfloat16)
    total_points = points * points
    twist_index = counter[:, None] * counter[None, :] % total_points
    twist_angle = 2.0 * math.pi / total_points * twist_index.astype(jnp.float32)
    return (matrix, jnp.cos(twist_angle), direction * jnp.sin(twist_angle))


def transform(values, tables):
    matrix, twist_real, twist_imag = tables
    points = matrix.shape[1]
    leading = values.shape[:-3]
    grid_values = values.reshape((-1, 2, points, points))
    segmented = jnp.einsum(
        "nrab,rasc->nscb", grid_values, matrix, preferred_element_type=jnp.float32
    )
    real_part = segmented[:, 0]
    imag_part = segmented[:, 1]
    turned = jnp.stack(
        [
            real_part * twist_real - imag_part * twist_imag,
            real_part * twist_imag + imag_part * twist_real,
        ],
        axis=1,
    ).astype(jnp.bfloat16)
    result = jnp.einsum("nscb,sbtd->ntdc", turned, matrix, preferred_element_type=jnp.float32)
    return result.reshape(leading + (2, points, points))


def complex_times(first, second):
    real_part = first[..., 0, :, :] * second[..., 0, :, :] - first[..., 1, :, :] * second[..., 1, :, :]
    imag_part = first[..., 0, :, :] * second[..., 1, :, :] + first[..., 1, :, :] * second[..., 0, :, :]
    return jnp.stack([real_part, imag_part], axis=-3)


def conjugate(values):
    return jnp.stack([values[..., 0, :, :], -values[..., 1, :, :]], axis=-3)


def propagate(values, spectrum, forward, inverse):
    moved_on = transform(values.astype(jnp.bfloat16), forward)
    return transform(complex_times(moved_on, spectrum).astype(jnp.bfloat16), inverse)


def propagator(wave_nums, points_all):
    counter = jnp.arange(points_all, dtype=jnp.int32)
    folded = jnp.where(counter < points_all // 2, counter, counter - points_all).astype(jnp.float32)
    lateral = 2.0 * math.pi / points_all * folded
    excess = wave_nums[:, None] ** 2 - lateral[None, :] ** 2
    upward = jnp.sqrt(jnp.maximum(excess, 0.0)) * STEP_DEPTH
    damped = jnp.sqrt(jnp.maximum(-excess, 0.0)) * STEP_DEPTH
    real_part = jnp.where(excess > 0, jnp.cos(upward), jnp.exp(-damped))
    imag_part = jnp.where(excess > 0, jnp.sin(upward), jnp.zeros_like(upward))
    return jnp.stack([real_part, imag_part], axis=1)


def screens(wave_nums, slowness):
    phase = wave_nums[:, None, None] * STEP_DEPTH * slowness[None]
    return jnp.stack([jnp.cos(phase), jnp.sin(phase)], axis=2)


def encoded_sources(incident, encode, sources):
    shifts = jnp.arange(sources, dtype=jnp.int32)
    bit_set = encode[:, None] >> shifts[None, :] & 1
    signs_all = (1 - 2 * bit_set).astype(jnp.float32)
    return jnp.sum(signs_all[:, :, None, None] * incident, axis=1)


def lookup_waves(freq_index, wavenum, table_size):
    onehot_rows = (freq_index[:, None] == jnp.arange(table_size, dtype=jnp.int32)[None, :]).astype(
        jnp.float32
    )
    return jnp.sum(onehot_rows * wavenum[None, :], axis=1)


def gram_sum_kernel(stages, part_ref, out_ref, *scratch):
    count = len(stages)
    slots = scratch[:count]
    send_sems, recv_sems, carried = scratch[count], scratch[count + 1], scratch[count + 2]
    barrier = pltpu.get_barrier_semaphore()
    peers_total = 0
    for axis, size in stages:
        me = lax.axis_index(axis)
        for step in range(1, size):
            pl.semaphore_signal(barrier, inc=1, device_id={axis: lax.rem(me + step, size)},
                                device_id_type=pl.DeviceIdType.MESH)
            peers_total += 1
    pl.semaphore_wait(barrier, peers_total)
    carried[...] = part_ref[...]
    used = 0
    offset = 0
    for stage, (axis, size) in enumerate(stages):
        me = lax.axis_index(axis)
        slot = slots[stage]
        copies = []
        for step in range(1, size):
            copy = pltpu.make_async_remote_copy(
                src_ref=carried,
                dst_ref=slot.at[me],
                send_sem=send_sems.at[used + step - 1],
                recv_sem=recv_sems.at[offset + me],
                device_id={axis: lax.rem(me + step, size)},
                device_id_type=pl.DeviceIdType.MESH,
            )
            copy.start()
            copies.append(copy)
        slot[me] = carried[...]
        for copy in copies:
            copy.wait_send()
        for step in range(1, size):
            sender = lax.rem(me + size - step, size)
            incoming = pltpu.make_async_remote_copy(
                src_ref=carried,
                dst_ref=slot.at[sender],
                send_sem=send_sems.at[used + step - 1],
                recv_sem=recv_sems.at[offset + sender],
                device_id={axis: lax.rem(me + step, size)},
                device_id_type=pl.DeviceIdType.MESH,
            )
            incoming.wait_recv()
        used += size - 1
        offset += size
        total = slot[0]
        for member in range(1, size):
            total = total + slot[member]
        carried[...] = total
    out_ref[...] = carried[...]


def gram_sum(part, stages):
    stages = [(axis, size) for axis, size in stages if size > 1]
    sends = sum(size - 1 for _, size in stages)
    scratch = [pltpu.VMEM((size,) + part.shape, jnp.float32) for _, size in stages]
    scratch += [
        pltpu.SemaphoreType.DMA((max(sends, 1),)),
        pltpu.SemaphoreType.DMA((max(sum(size for _, size in stages), 1),)),
        pltpu.VMEM(part.shape, jnp.float32),
    ]
    return pl.pallas_call(
        lambda *refs: gram_sum_kernel(stages, *refs),
        out_shape=jax.ShapeDtypeStruct(part.shape, jnp.float32),
        in_specs=[pl.BlockSpec(memory_space=pltpu.VMEM)],
        out_specs=pl.BlockSpec(memory_space=pltpu.VMEM),
        scratch_shapes=scratch,
        compiler_params=pltpu.CompilerParams(collective_id=0, has_side_effects=True),
    )(part)


def exchange(axis, size, current, slot, send_sems, recv_sems, offset, whole=False):
    me = lax.axis_index(axis)
    copies = []
    for step in range(1, size):
        peer = lax.rem(me + step, size)
        copy = pltpu.make_async_remote_copy(
            src_ref=current if whole else current.at[peer],
            dst_ref=slot.at[me],
            send_sem=send_sems.at[offset + peer],
            recv_sem=recv_sems.at[offset + me],
            device_id={axis: peer},
            device_id_type=pl.DeviceIdType.MESH,
        )
        copy.start()
        copies.append(copy)
    for copy in copies:
        copy.wait_send()
    for step in range(1, size):
        sender = lax.rem(me + size - step, size)
        incoming = pltpu.make_async_remote_copy(
            src_ref=current if whole else current.at[sender],
            dst_ref=slot.at[sender],
            send_sem=send_sems.at[offset + sender],
            recv_sem=recv_sems.at[offset + sender],
            device_id={axis: sender},
            device_id_type=pl.DeviceIdType.MESH,
        )
        incoming.wait_recv()
    return me


def scatter_kernel(stages, part_ref, extra_ref, out_ref, *scratch):
    count = len(stages)
    slots = scratch[:count]
    sums = scratch[count : 2 * count - 1]
    mine, gathered, send_sems, recv_sems = scratch[2 * count - 1 :]
    barrier = pltpu.get_barrier_semaphore()
    peers_total = 0
    for axis, size in stages + [("depth", out_ref.shape[0])]:
        me = lax.axis_index(axis)
        for step in range(1, size):
            pl.semaphore_signal(barrier, inc=1, device_id={axis: lax.rem(me + step, size)},
                                device_id_type=pl.DeviceIdType.MESH)
            peers_total += 1
    pl.semaphore_wait(barrier, peers_total)
    current = part_ref
    offset = 0
    for stage, (axis, size) in enumerate(stages):
        me = exchange(axis, size, current, slots[stage], send_sems, recv_sems, offset)
        offset += size
        total = current[me]
        for step in range(1, size):
            total = total + slots[stage][lax.rem(me + size - step, size)]
        if stage + 1 < count:
            sums[stage][...] = total
            current = sums[stage]
        else:
            mine[0] = total
    mine[1] = extra_ref[...]
    depth_size = out_ref.shape[0]
    me = exchange("depth", depth_size, mine, gathered, send_sems, recv_sems, offset, whole=True)
    gathered[me] = mine[...]
    out_ref[...] = gathered[...]


def scatter_gather(part, extra, stages, depth_size):
    stages = [(axis, size) for axis, size in stages if size > 1]
    part = part.reshape(tuple(size for _, size in stages) + part.shape[-2:])
    scratch = [pltpu.VMEM(part.shape[stage:], jnp.float32) for stage in range(len(stages))]
    scratch += [pltpu.VMEM(part.shape[stage + 1 :], jnp.float32) for stage in range(len(stages) - 1)]
    block = (2,) + extra.shape
    scratch += [
        pltpu.VMEM(block, jnp.float32),
        pltpu.VMEM((depth_size,) + block, jnp.float32),
        pltpu.SemaphoreType.DMA((sum(size for _, size in stages) + depth_size,)),
        pltpu.SemaphoreType.DMA((sum(size for _, size in stages) + depth_size,)),
    ]
    return pl.pallas_call(
        lambda *refs: scatter_kernel(stages, *refs),
        out_shape=jax.ShapeDtypeStruct((depth_size,) + block, jnp.float32),
        in_specs=[pl.BlockSpec(memory_space=pltpu.VMEM)] * 2,
        out_specs=pl.BlockSpec(memory_space=pltpu.VMEM),
        scratch_shapes=scratch,
        compiler_params=pltpu.CompilerParams(collective_id=1, has_side_effects=True),
    )(part, extra)


def shards(incident, encode, freq_index, wavenum, slowness, probes):
    points_all = SIDE * SIDE
    forward = dft_tables(SIDE, -1.0)
    inverse = dft_tables(SIDE, 1.0)
    group_count = incident.shape[0]
    probe_count = probes.shape[0]
    src_count = lax.axis_size(SRC_AXES)
    depth_count = lax.axis_size("depth")
    spread = jnp.broadcast_to(slowness[None], (depth_count,) + slowness.shape)
    slowness_all = lax.all_to_all(spread, "depth", 0, 0, tiled=True).reshape(-1, slowness.shape[-1])
    plane_count = slowness_all.shape[0]
    probe_mine = lax.all_to_all(probes, "depth", 0, 1, tiled=True).astype(jnp.float32)
    probe_mine = probe_mine.reshape(probe_mine.shape[:2] + (SIDE, SIDE))
    sources = encoded_sources(incident, encode, incident.shape[1])
    sources = sources.reshape(sources.shape[:-1] + (SIDE, SIDE))
    wave_nums = lookup_waves(freq_index, wavenum, wavenum.shape[0])
    spectra = propagator(wave_nums, points_all)
    spectra = spectra.reshape(spectra.shape[:-1] + (SIDE, SIDE))
    spectra_back = conjugate(spectra)
    plane_screens = screens(wave_nums, slowness_all)
    plane_screens = plane_screens.reshape(plane_screens.shape[:-1] + (SIDE, SIDE))
    born_scale = wave_nums * STEP_DEPTH

    fields = []
    current = sources
    for plane in range(plane_count):
        current = complex_times(plane_screens[:, plane], propagate(current, spectra, forward, inverse))
        fields.append(current)

    def born(plane):
        scaled = born_scale[:, None, None, None] * probe_mine[None, :, plane]
        background = fields[plane]
        return jnp.stack([-scaled * background[:, None, 1], scaled * background[:, None, 0]], axis=2)

    tangent = born(0)
    for plane in range(1, plane_count):
        moved_on = complex_times(
            plane_screens[:, plane][:, None], propagate(tangent, spectra[:, None], forward, inverse)
        )
        tangent = moved_on + born(plane)

    adjoint = tangent
    pieces = [None] * plane_count
    for plane in reversed(range(plane_count)):
        background = fields[plane]
        product_terms = born_scale[:, None, None, None] * (
            background[:, None, 0] * adjoint[:, :, 1] - background[:, None, 1] * adjoint[:, :, 0]
        )
        pieces[plane] = jnp.sum(product_terms, axis=0)
        if plane > 0:
            turned_back = complex_times(conjugate(plane_screens[:, plane])[:, None], adjoint)
            adjoint = propagate(turned_back, spectra_back[:, None], forward, inverse)
    sketch_part = jnp.stack(pieces, axis=1)
    rows, planes = sketch_part.shape[0], sketch_part.shape[1]
    by_axes = sketch_part.reshape(rows, planes, CHIPS_Y, CHIPS_Z, CORES, -1)
    slab_width = by_axes.shape[-1]
    by_axes = jnp.transpose(by_axes, (4, 3, 2, 0, 1, 5)).reshape(
        CORES, CHIPS_Z, CHIPS_Y, rows, planes * slab_width
    )
    src_index = lax.axis_index(SRC_AXES)
    probe_slab = lax.dynamic_slice_in_dim(probes, src_index * slab_width, slab_width, 2)
    probe_slab = jnp.transpose(probe_slab.reshape(depth_count, rows, slab_width), (1, 0, 2))
    probe_slab = probe_slab.reshape(rows, depth_count * slab_width).astype(jnp.float32)
    stage_sizes = [("core", CORES), ("chip_z", CHIPS_Z), ("chip_y", CHIPS_Y)]
    both = scatter_gather(by_axes, probe_slab, stage_sizes, depth_count)
    summed = both[:, 0].reshape(probe_count, planes, slab_width)
    local_probes = jnp.transpose(
        both[:, 1].reshape(depth_count, rows, depth_count, slab_width), (2, 1, 0, 3)
    ).reshape(probe_count, planes, slab_width)
    sketch_all = summed / (group_count * src_count) + DAMPING * local_probes
    flattened_all = sketch_all.reshape(probe_count, -1)
    row_total = flattened_all.shape[1] * src_count
    gram_local = jnp.dot(flattened_all, flattened_all.T, precision=lax.Precision.HIGHEST) / row_total
    stage_sizes = [(axis, lax.axis_size(axis)) for axis in ("core", "chip_z", "chip_y")]
    gram_matrix = gram_sum(gram_local, stage_sizes)
    sketch = lax.dynamic_slice_in_dim(sketch_all, lax.axis_index("depth"), 1, 1)
    local_planes = 1
    flattened = sketch.reshape(probe_count, local_planes * slab_width)
    lower_factor = jnp.linalg.cholesky(gram_matrix)
    identity = jnp.eye(probe_count, dtype=jnp.float32)
    inverse_lower = lax.linalg.triangular_solve(lower_factor, identity, left_side=True, lower=True)
    sketch_basis = jnp.dot(inverse_lower, flattened, precision=lax.Precision.HIGHEST).reshape(
        probe_count, local_planes, slab_width
    )
    return (sketch_basis, lower_factor.T)


def solution(mesh):
    src_size, depth_size = mesh.devices.shape
    cut = mesh.devices.reshape(CHIPS_Y, CHIPS_Z, CORES, depth_size)
    fine = Mesh(cut, SRC_AXES + ("depth",))
    in_specs = (
        P(SRC_AXES, None, None, None),
        P(SRC_AXES),
        P(SRC_AXES),
        P(),
        P("depth", None),
        P(None, "depth", None),
    )
    out_specs = (P(None, "depth", SRC_AXES), P())
    return jax.shard_map(shards, mesh=fine, in_specs=in_specs, out_specs=out_specs, check_vma=False)
```

```python
import math

import jax
import jax.numpy as jnp
from jax import lax
from jax.experimental import pallas as pl
from jax.experimental.pallas import tpu as pltpu
from jax.sharding import Mesh, PartitionSpec as P

SIDE = 64
CHIPS_Y = 8
CHIPS_Z = 8
CORES = 2
SRC_AXES = ("chip_y", "chip_z", "core")


DAMPING = 0.5
STEP_DEPTH = 1.0


def dft_tables(points, direction):
    counter = jnp.arange(points, dtype=jnp.int32)
    product = counter[:, None] * counter[None, :] % points
    angles = 2.0 * math.pi / points * product.astype(jnp.float32)
    cosine = jnp.cos(angles) / math.sqrt(points)
    sine_part = direction * jnp.sin(angles) / math.sqrt(points)
    matrix = jnp.stack(
        [jnp.stack([cosine, sine_part], axis=1), jnp.stack([-sine_part, cosine], axis=1)], axis=0
    )
    matrix = matrix.astype(jnp.bfloat16)
    total_points = points * points
    twist_index = counter[:, None] * counter[None, :] % total_points
    twist_angle = 2.0 * math.pi / total_points * twist_index.astype(jnp.float32)
    return (matrix, jnp.cos(twist_angle), direction * jnp.sin(twist_angle))


def transform(values, tables):
    matrix, twist_real, twist_imag = tables
    points = matrix.shape[1]
    leading = values.shape[:-3]
    grid_values = values.reshape((-1, 2, points, points))
    segmented = jnp.einsum(
        "nrab,rasc->nscb", grid_values, matrix, preferred_element_type=jnp.float32
    )
    real_part = segmented[:, 0]
    imag_part = segmented[:, 1]
    turned = jnp.stack(
        [
            real_part * twist_real - imag_part * twist_imag,
            real_part * twist_imag + imag_part * twist_real,
        ],
        axis=1,
    ).astype(jnp.bfloat16)
    result = jnp.einsum("nscb,sbtd->ntdc", turned, matrix, preferred_element_type=jnp.float32)
    return result.reshape(leading + (2, points, points))


def complex_times(first, second):
    real_part = first[..., 0, :, :] * second[..., 0, :, :] - first[..., 1, :, :] * second[..., 1, :, :]
    imag_part = first[..., 0, :, :] * second[..., 1, :, :] + first[..., 1, :, :] * second[..., 0, :, :]
    return jnp.stack([real_part, imag_part], axis=-3)


def conjugate(values):
    return jnp.stack([values[..., 0, :, :], -values[..., 1, :, :]], axis=-3)


def propagate(values, spectrum, forward, inverse):
    moved_on = transform(values.astype(jnp.bfloat16), forward)
    return transform(complex_times(moved_on, spectrum).astype(jnp.bfloat16), inverse)


def propagator(wave_nums, points_all):
    counter = jnp.arange(points_all, dtype=jnp.int32)
    folded = jnp.where(counter < points_all // 2, counter, counter - points_all).astype(jnp.float32)
    lateral = 2.0 * math.pi / points_all * folded
    excess = wave_nums[:, None] ** 2 - lateral[None, :] ** 2
    upward = jnp.sqrt(jnp.maximum(excess, 0.0)) * STEP_DEPTH
    damped = jnp.sqrt(jnp.maximum(-excess, 0.0)) * STEP_DEPTH
    real_part = jnp.where(excess > 0, jnp.cos(upward), jnp.exp(-damped))
    imag_part = jnp.where(excess > 0, jnp.sin(upward), jnp.zeros_like(upward))
    return jnp.stack([real_part, imag_part], axis=1)


def screens(wave_nums, slowness):
    phase = wave_nums[:, None, None] * STEP_DEPTH * slowness[None]
    return jnp.stack([jnp.cos(phase), jnp.sin(phase)], axis=2)


def encoded_sources(incident, encode, sources):
    shifts = jnp.arange(sources, dtype=jnp.int32)
    bit_set = encode[:, None] >> shifts[None, :] & 1
    signs_all = (1 - 2 * bit_set).astype(jnp.float32)
    return jnp.sum(signs_all[:, :, None, None] * incident, axis=1)


def lookup_waves(freq_index, wavenum, table_size):
    onehot_rows = (freq_index[:, None] == jnp.arange(table_size, dtype=jnp.int32)[None, :]).astype(
        jnp.float32
    )
    return jnp.sum(onehot_rows * wavenum[None, :], axis=1)


def exchange(axis, size, current, slot, send_sems, recv_sems, offset, whole=False):
    me = lax.axis_index(axis)
    copies = []
    for step in range(1, size):
        peer = lax.rem(me + step, size)
        copy = pltpu.make_async_remote_copy(
            src_ref=current if whole else current.at[peer],
            dst_ref=slot.at[me],
            send_sem=send_sems.at[offset + peer],
            recv_sem=recv_sems.at[offset + me],
            device_id={axis: peer},
            device_id_type=pl.DeviceIdType.MESH,
        )
        copy.start()
        copies.append(copy)
    for copy in copies:
        copy.wait_send()
    for step in range(1, size):
        sender = lax.rem(me + size - step, size)
        incoming = pltpu.make_async_remote_copy(
            src_ref=current if whole else current.at[sender],
            dst_ref=slot.at[sender],
            send_sem=send_sems.at[offset + sender],
            recv_sem=recv_sems.at[offset + sender],
            device_id={axis: sender},
            device_id_type=pl.DeviceIdType.MESH,
        )
        incoming.wait_recv()
    return me


def reduce_kernel(stages, depth_size, divisor, row_total, part_ref, probe_ref, sketch_ref, gram_ref,
                  *scratch):
    count = len(stages)
    slots = scratch[:count]
    sums = scratch[count : 2 * count - 1]
    gram_slots = scratch[2 * count - 1 : 3 * count - 1]
    mine, gathered, carried, send_sems, recv_sems = scratch[3 * count - 1 :]
    barrier = pltpu.get_barrier_semaphore()
    peers_total = 0
    for axis, size in stages + [("depth", depth_size)]:
        me = lax.axis_index(axis)
        for step in range(1, size):
            pl.semaphore_signal(barrier, inc=1, device_id={axis: lax.rem(me + step, size)},
                                device_id_type=pl.DeviceIdType.MESH)
            peers_total += 1
    pl.semaphore_wait(barrier, peers_total)
    current = part_ref
    offset = 0
    for stage, (axis, size) in enumerate(stages):
        me = exchange(axis, size, current, slots[stage], send_sems, recv_sems, offset)
        offset += size
        total = current[me]
        for step in range(1, size):
            total = total + slots[stage][lax.rem(me + size - step, size)]
        if stage + 1 < count:
            sums[stage][...] = total
            current = sums[stage]
        else:
            mine[...] = total
    me = exchange("depth", depth_size, mine, gathered, send_sems, recv_sems, offset, whole=True)
    offset += depth_size
    gathered[me] = mine[...]
    summed = gathered[...].reshape(sketch_ref.shape)
    sketch = summed / divisor + DAMPING * probe_ref[...]
    sketch_ref[...] = sketch
    carried[...] = lax.dot_general(
        sketch, sketch, (((1,), (1,)), ((), ())), precision=lax.Precision.HIGHEST,
        preferred_element_type=jnp.float32,
    ) / row_total
    for stage, (axis, size) in enumerate(stages):
        slot = gram_slots[stage]
        me = exchange(axis, size, carried, slot, send_sems, recv_sems, offset, whole=True)
        offset += size
        slot[me] = carried[...]
        total = slot[0]
        for member in range(1, size):
            total = total + slot[member]
        carried[...] = total
    gram_ref[...] = carried[...]


def reduce_all(part, probe_all, stages, depth_size, divisor, row_total):
    stages = [(axis, size) for axis, size in stages if size > 1]
    part = part.reshape(tuple(size for _, size in stages) + part.shape[-2:])
    rows, width = probe_all.shape
    scratch = [pltpu.VMEM(part.shape[stage:], jnp.float32) for stage in range(len(stages))]
    scratch += [pltpu.VMEM(part.shape[stage + 1 :], jnp.float32) for stage in range(len(stages) - 1)]
    scratch += [pltpu.VMEM((size, rows, rows), jnp.float32) for _, size in stages]
    semaphores = 2 * sum(size for _, size in stages) + depth_size
    scratch += [
        pltpu.VMEM(part.shape[-2:], jnp.float32),
        pltpu.VMEM((depth_size,) + part.shape[-2:], jnp.float32),
        pltpu.VMEM((rows, rows), jnp.float32),
        pltpu.SemaphoreType.DMA((semaphores,)),
        pltpu.SemaphoreType.DMA((semaphores,)),
    ]
    return pl.pallas_call(
        lambda *refs: reduce_kernel(stages, depth_size, divisor, row_total, *refs),
        out_shape=(
            jax.ShapeDtypeStruct((rows, width), jnp.float32),
            jax.ShapeDtypeStruct((rows, rows), jnp.float32),
        ),
        in_specs=[pl.BlockSpec(memory_space=pltpu.VMEM)] * 2,
        out_specs=(pl.BlockSpec(memory_space=pltpu.VMEM), pl.BlockSpec(memory_space=pltpu.VMEM)),
        scratch_shapes=scratch,
        compiler_params=pltpu.CompilerParams(collective_id=2, has_side_effects=True),
    )(part, probe_all)


def shards(incident, encode, freq_index, wavenum, slowness, probes):
    points_all = SIDE * SIDE
    forward = dft_tables(SIDE, -1.0)
    inverse = dft_tables(SIDE, 1.0)
    group_count = incident.shape[0]
    probe_count = probes.shape[0]
    src_count = lax.axis_size(SRC_AXES)
    depth_count = lax.axis_size("depth")
    spread = jnp.broadcast_to(slowness[None], (depth_count,) + slowness.shape)
    slowness_all = lax.all_to_all(spread, "depth", 0, 0, tiled=True).reshape(-1, slowness.shape[-1])
    plane_count = slowness_all.shape[0]
    probe_mine = lax.all_to_all(probes, "depth", 0, 1, tiled=True).astype(jnp.float32)
    probe_mine = probe_mine.reshape(probe_mine.shape[:2] + (SIDE, SIDE))
    slab_points = probes.shape[2] // src_count
    probe_slab = lax.dynamic_slice_in_dim(
        probes, lax.axis_index(SRC_AXES) * slab_points, slab_points, 2
    )
    probe_slab = jnp.broadcast_to(probe_slab[None], (depth_count,) + probe_slab.shape)
    probe_slab = lax.all_to_all(probe_slab, "depth", 0, 0, tiled=True)
    probe_all = jnp.transpose(probe_slab[:, :, 0], (1, 0, 2)).reshape(probe_count, -1)
    probe_all = probe_all.astype(jnp.float32)
    sources = encoded_sources(incident, encode, incident.shape[1])
    sources = sources.reshape(sources.shape[:-1] + (SIDE, SIDE))
    wave_nums = lookup_waves(freq_index, wavenum, wavenum.shape[0])
    spectra = propagator(wave_nums, points_all)
    spectra = spectra.reshape(spectra.shape[:-1] + (SIDE, SIDE))
    spectra_back = conjugate(spectra)
    plane_screens = screens(wave_nums, slowness_all)
    plane_screens = plane_screens.reshape(plane_screens.shape[:-1] + (SIDE, SIDE))
    born_scale = wave_nums * STEP_DEPTH

    fields = []
    current = sources
    for plane in range(plane_count):
        current = complex_times(plane_screens[:, plane], propagate(current, spectra, forward, inverse))
        fields.append(current)

    def born(plane):
        scaled = born_scale[:, None, None, None] * probe_mine[None, :, plane]
        background = fields[plane]
        return jnp.stack([-scaled * background[:, None, 1], scaled * background[:, None, 0]], axis=2)

    tangent = born(0)
    for plane in range(1, plane_count):
        moved_on = complex_times(
            plane_screens[:, plane][:, None], propagate(tangent, spectra[:, None], forward, inverse)
        )
        tangent = moved_on + born(plane)

    adjoint = tangent
    pieces = [None] * plane_count
    for plane in reversed(range(plane_count)):
        background = fields[plane]
        product_terms = born_scale[:, None, None, None] * (
            background[:, None, 0] * adjoint[:, :, 1] - background[:, None, 1] * adjoint[:, :, 0]
        )
        pieces[plane] = jnp.sum(product_terms, axis=0)
        if plane > 0:
            turned_back = complex_times(conjugate(plane_screens[:, plane])[:, None], adjoint)
            adjoint = propagate(turned_back, spectra_back[:, None], forward, inverse)
    sketch_part = jnp.stack(pieces, axis=1)
    rows, planes = sketch_part.shape[0], sketch_part.shape[1]
    by_axes = sketch_part.reshape(rows, planes, CHIPS_Y, CHIPS_Z, CORES, -1)
    slab_width = by_axes.shape[-1]
    by_axes = jnp.transpose(by_axes, (4, 3, 2, 0, 1, 5)).reshape(
        CORES, CHIPS_Z, CHIPS_Y, rows, planes * slab_width
    )
    stage_sizes = [("core", CORES), ("chip_z", CHIPS_Z), ("chip_y", CHIPS_Y)]
    row_total = planes * slab_width * src_count
    sketch_all, gram_matrix = reduce_all(
        by_axes, probe_all, stage_sizes, depth_count, group_count * src_count, row_total
    )
    depth_index = lax.axis_index("depth")
    flattened = lax.dynamic_slice_in_dim(sketch_all, depth_index * slab_width, slab_width, 1)
    local_planes = 1
    lower_factor = jnp.linalg.cholesky(gram_matrix)
    identity = jnp.eye(probe_count, dtype=jnp.float32)
    inverse_lower = lax.linalg.triangular_solve(lower_factor, identity, left_side=True, lower=True)
    sketch_basis = jnp.dot(inverse_lower, flattened, precision=lax.Precision.HIGHEST).reshape(
        probe_count, local_planes, slab_width
    )
    return (sketch_basis, lower_factor.T)


def solution(mesh):
    src_size, depth_size = mesh.devices.shape
    cut = mesh.devices.reshape(CHIPS_Y, CHIPS_Z, CORES, depth_size)
    fine = Mesh(cut, SRC_AXES + ("depth",))
    in_specs = (
        P(SRC_AXES, None, None, None),
        P(SRC_AXES),
        P(SRC_AXES),
        P(),
        P("depth", None),
        P(None, "depth", None),
    )
    out_specs = (P(None, "depth", SRC_AXES), P())
    return jax.shard_map(shards, mesh=fine, in_specs=in_specs, out_specs=out_specs, check_vma=False)
```

```python
import math

import jax
import jax.numpy as jnp
from jax import lax
from jax.experimental import pallas as pl
from jax.experimental.pallas import tpu as pltpu
from jax.sharding import Mesh, PartitionSpec as P

SIDE = 64
CHIPS_Y = 8
CHIPS_Z = 8
CORES = 2
SRC_AXES = ("chip_y", "chip_z", "core")


DAMPING = 0.5
STEP_DEPTH = 1.0


def dft_tables(points, direction):
    counter = jnp.arange(points, dtype=jnp.int32)
    product = counter[:, None] * counter[None, :] % points
    angles = 2.0 * math.pi / points * product.astype(jnp.float32)
    cosine = jnp.cos(angles) / math.sqrt(points)
    sine_part = direction * jnp.sin(angles) / math.sqrt(points)
    matrix = jnp.stack(
        [jnp.stack([cosine, sine_part], axis=1), jnp.stack([-sine_part, cosine], axis=1)], axis=0
    )
    matrix = matrix.astype(jnp.bfloat16)
    total_points = points * points
    twist_index = counter[:, None] * counter[None, :] % total_points
    twist_angle = 2.0 * math.pi / total_points * twist_index.astype(jnp.float32)
    return (matrix, jnp.cos(twist_angle), direction * jnp.sin(twist_angle))


def transform(values, tables):
    matrix, twist_real, twist_imag = tables
    points = matrix.shape[1]
    leading = values.shape[:-3]
    grid_values = values.reshape((-1, 2, points, points))
    segmented = jnp.einsum(
        "nrab,rasc->nscb", grid_values, matrix, preferred_element_type=jnp.float32
    )
    real_part = segmented[:, 0]
    imag_part = segmented[:, 1]
    turned = jnp.stack(
        [
            real_part * twist_real - imag_part * twist_imag,
            real_part * twist_imag + imag_part * twist_real,
        ],
        axis=1,
    ).astype(jnp.bfloat16)
    result = jnp.einsum("nscb,sbtd->ntdc", turned, matrix, preferred_element_type=jnp.float32)
    return result.reshape(leading + (2, points, points))


def complex_times(first, second):
    real_part = first[..., 0, :, :] * second[..., 0, :, :] - first[..., 1, :, :] * second[..., 1, :, :]
    imag_part = first[..., 0, :, :] * second[..., 1, :, :] + first[..., 1, :, :] * second[..., 0, :, :]
    return jnp.stack([real_part, imag_part], axis=-3)


def conjugate(values):
    return jnp.stack([values[..., 0, :, :], -values[..., 1, :, :]], axis=-3)


def propagate(values, spectrum, forward, inverse):
    moved_on = transform(values.astype(jnp.bfloat16), forward)
    return transform(complex_times(moved_on, spectrum).astype(jnp.bfloat16), inverse)


def propagator(wave_nums, points_all):
    counter = jnp.arange(points_all, dtype=jnp.int32)
    folded = jnp.where(counter < points_all // 2, counter, counter - points_all).astype(jnp.float32)
    lateral = 2.0 * math.pi / points_all * folded
    excess = wave_nums[:, None] ** 2 - lateral[None, :] ** 2
    upward = jnp.sqrt(jnp.maximum(excess, 0.0)) * STEP_DEPTH
    damped = jnp.sqrt(jnp.maximum(-excess, 0.0)) * STEP_DEPTH
    real_part = jnp.where(excess > 0, jnp.cos(upward), jnp.exp(-damped))
    imag_part = jnp.where(excess > 0, jnp.sin(upward), jnp.zeros_like(upward))
    return jnp.stack([real_part, imag_part], axis=1)


def screens(wave_nums, slowness):
    phase = wave_nums[:, None, None] * STEP_DEPTH * slowness[None]
    return jnp.stack([jnp.cos(phase), jnp.sin(phase)], axis=2)


def encoded_sources(incident, encode, sources):
    shifts = jnp.arange(sources, dtype=jnp.int32)
    bit_set = encode[:, None] >> shifts[None, :] & 1
    signs_all = (1 - 2 * bit_set).astype(jnp.float32)
    return jnp.sum(signs_all[:, :, None, None] * incident, axis=1)


def lookup_waves(freq_index, wavenum, table_size):
    onehot_rows = (freq_index[:, None] == jnp.arange(table_size, dtype=jnp.int32)[None, :]).astype(
        jnp.float32
    )
    return jnp.sum(onehot_rows * wavenum[None, :], axis=1)


def exchange(axis, size, current, slot, send_sems, recv_sems, offset, whole=False):
    me = lax.axis_index(axis)
    copies = []
    for step in range(1, size):
        peer = lax.rem(me + step, size)
        copy = pltpu.make_async_remote_copy(
            src_ref=current if whole else current.at[peer],
            dst_ref=slot.at[me],
            send_sem=send_sems.at[offset + peer],
            recv_sem=recv_sems.at[offset + me],
            device_id={axis: peer},
            device_id_type=pl.DeviceIdType.MESH,
        )
        copy.start()
        copies.append(copy)
    for copy in copies:
        copy.wait_send()
    for step in range(1, size):
        sender = lax.rem(me + size - step, size)
        incoming = pltpu.make_async_remote_copy(
            src_ref=current if whole else current.at[sender],
            dst_ref=slot.at[sender],
            send_sem=send_sems.at[offset + sender],
            recv_sem=recv_sems.at[offset + sender],
            device_id={axis: sender},
            device_id_type=pl.DeviceIdType.MESH,
        )
        incoming.wait_recv()
    return me


def reduce_kernel(stages, depth_size, divisor, row_total, part_ref, probe_ref, sketch_ref, gram_ref,
                  *scratch):
    count = len(stages)
    slots = scratch[:count]
    sums = scratch[count : 2 * count - 1]
    gram_slots = scratch[2 * count - 1 : 3 * count - 1]
    mine, gathered, carried, send_sems, recv_sems = scratch[3 * count - 1 :]
    barrier = pltpu.get_barrier_semaphore()
    peers_total = 0
    for axis, size in stages + [("depth", depth_size)]:
        me = lax.axis_index(axis)
        for step in range(1, size):
            pl.semaphore_signal(barrier, inc=1, device_id={axis: lax.rem(me + step, size)},
                                device_id_type=pl.DeviceIdType.MESH)
            peers_total += 1
    pl.semaphore_wait(barrier, peers_total)
    current = part_ref
    offset = 0
    for stage, (axis, size) in enumerate(stages):
        me = exchange(axis, size, current, slots[stage], send_sems, recv_sems, offset)
        offset += size
        total = current[me]
        for step in range(1, size):
            total = total + slots[stage][lax.rem(me + size - step, size)]
        if stage + 1 < count:
            sums[stage][...] = total
            current = sums[stage]
        else:
            mine[...] = total
    me = exchange("depth", depth_size, mine, gathered, send_sems, recv_sems, offset, whole=True)
    offset += depth_size
    gathered[me] = mine[...]
    summed = gathered[...].reshape(sketch_ref.shape)
    sketch = summed / divisor + DAMPING * probe_ref[...]
    sketch_ref[...] = sketch
    carried[...] = lax.dot_general(
        sketch, sketch, (((1,), (1,)), ((), ())), precision=lax.Precision.HIGHEST,
        preferred_element_type=jnp.float32,
    ) / row_total
    for stage, (axis, size) in enumerate(stages):
        slot = gram_slots[stage]
        me = exchange(axis, size, carried, slot, send_sems, recv_sems, offset, whole=True)
        offset += size
        slot[me] = carried[...]
        total = slot[0]
        for member in range(1, size):
            total = total + slot[member]
        carried[...] = total
    gram_ref[...] = carried[...]


def reduce_all(part, probe_all, stages, depth_size, divisor, row_total):
    stages = [(axis, size) for axis, size in stages if size > 1]
    part = part.reshape(tuple(size for _, size in stages) + part.shape[-2:])
    rows, width = probe_all.shape
    scratch = [pltpu.VMEM(part.shape[stage:], jnp.float32) for stage in range(len(stages))]
    scratch += [pltpu.VMEM(part.shape[stage + 1 :], jnp.float32) for stage in range(len(stages) - 1)]
    scratch += [pltpu.VMEM((size, rows, rows), jnp.float32) for _, size in stages]
    semaphores = 2 * sum(size for _, size in stages) + depth_size
    scratch += [
        pltpu.VMEM(part.shape[-2:], jnp.float32),
        pltpu.VMEM((depth_size,) + part.shape[-2:], jnp.float32),
        pltpu.VMEM((rows, rows), jnp.float32),
        pltpu.SemaphoreType.DMA((semaphores,)),
        pltpu.SemaphoreType.DMA((semaphores,)),
    ]
    return pl.pallas_call(
        lambda *refs: reduce_kernel(stages, depth_size, divisor, row_total, *refs),
        out_shape=(
            jax.ShapeDtypeStruct((rows, width), jnp.float32),
            jax.ShapeDtypeStruct((rows, rows), jnp.float32),
        ),
        in_specs=[pl.BlockSpec(memory_space=pltpu.VMEM)] * 2,
        out_specs=(pl.BlockSpec(memory_space=pltpu.VMEM), pl.BlockSpec(memory_space=pltpu.VMEM)),
        scratch_shapes=scratch,
        compiler_params=pltpu.CompilerParams(collective_id=2, has_side_effects=True),
    )(part, probe_all)


def shards(incident, encode, freq_index, wavenum, slowness, probes):
    points_all = SIDE * SIDE
    forward = dft_tables(SIDE, -1.0)
    inverse = dft_tables(SIDE, 1.0)
    group_count = incident.shape[0]
    probe_count = probes.shape[0]
    src_count = lax.axis_size(SRC_AXES)
    depth_count = lax.axis_size("depth")
    rows = probe_count // depth_count
    points = probes.shape[2]
    slab_points = points // src_count
    probe_slab = lax.dynamic_slice_in_dim(
        probes, lax.axis_index(SRC_AXES) * slab_points, slab_points, 2
    )
    high = slowness.astype(jnp.bfloat16)
    rest = slowness - high.astype(jnp.float32)
    middle = rest.astype(jnp.bfloat16)
    low = (rest - middle.astype(jnp.float32)).astype(jnp.bfloat16)
    shared = jnp.concatenate([probe_slab.reshape(-1), high.reshape(-1), middle.reshape(-1), low.reshape(-1)])
    payload = jnp.concatenate(
        [probes.reshape(depth_count, -1), jnp.broadcast_to(shared[None], (depth_count,) + shared.shape)],
        axis=1,
    )
    payload = lax.all_to_all(payload, "depth", 0, 0, tiled=True)
    cut = rows * points
    probe_mine = jnp.transpose(payload[:, :cut].reshape(depth_count, rows, points), (1, 0, 2))
    probe_mine = probe_mine.astype(jnp.float32)
    probe_mine = probe_mine.reshape(probe_mine.shape[:2] + (SIDE, SIDE))
    slab_size = probe_count * slab_points
    probe_all = payload[:, cut : cut + slab_size].reshape(depth_count, probe_count, slab_points)
    probe_all = jnp.transpose(probe_all, (1, 0, 2)).reshape(probe_count, -1).astype(jnp.float32)
    parts = payload[:, cut + slab_size :].reshape(depth_count, 3, points).astype(jnp.float32)
    slowness_all = (parts[:, 0] + parts[:, 1]) + parts[:, 2]
    plane_count = slowness_all.shape[0]
    sources = encoded_sources(incident, encode, incident.shape[1])
    sources = sources.reshape(sources.shape[:-1] + (SIDE, SIDE))
    wave_nums = lookup_waves(freq_index, wavenum, wavenum.shape[0])
    spectra = propagator(wave_nums, points_all)
    spectra = spectra.reshape(spectra.shape[:-1] + (SIDE, SIDE))
    spectra_back = conjugate(spectra)
    plane_screens = screens(wave_nums, slowness_all)
    plane_screens = plane_screens.reshape(plane_screens.shape[:-1] + (SIDE, SIDE))
    born_scale = wave_nums * STEP_DEPTH

    fields = []
    current = sources
    for plane in range(plane_count):
        current = complex_times(plane_screens[:, plane], propagate(current, spectra, forward, inverse))
        fields.append(current)

    def born(plane):
        scaled = born_scale[:, None, None, None] * probe_mine[None, :, plane]
        background = fields[plane]
        return jnp.stack([-scaled * background[:, None, 1], scaled * background[:, None, 0]], axis=2)

    tangent = born(0)
    for plane in range(1, plane_count):
        moved_on = complex_times(
            plane_screens[:, plane][:, None], propagate(tangent, spectra[:, None], forward, inverse)
        )
        tangent = moved_on + born(plane)

    adjoint = tangent
    pieces = [None] * plane_count
    for plane in reversed(range(plane_count)):
        background = fields[plane]
        product_terms = born_scale[:, None, None, None] * (
            background[:, None, 0] * adjoint[:, :, 1] - background[:, None, 1] * adjoint[:, :, 0]
        )
        pieces[plane] = jnp.sum(product_terms, axis=0)
        if plane > 0:
            turned_back = complex_times(conjugate(plane_screens[:, plane])[:, None], adjoint)
            adjoint = propagate(turned_back, spectra_back[:, None], forward, inverse)
    sketch_part = lax.optimization_barrier(jnp.stack(pieces, axis=1))
    rows, planes = sketch_part.shape[0], sketch_part.shape[1]
    by_axes = sketch_part.reshape(rows, planes, CHIPS_Y, CHIPS_Z, CORES, -1)
    slab_width = by_axes.shape[-1]
    by_axes = jnp.transpose(by_axes, (4, 3, 2, 0, 1, 5)).reshape(
        CORES, CHIPS_Z, CHIPS_Y, rows, planes * slab_width
    )
    stage_sizes = [("core", CORES), ("chip_z", CHIPS_Z), ("chip_y", CHIPS_Y)]
    row_total = planes * slab_width * src_count
    sketch_all, gram_matrix = reduce_all(
        by_axes, probe_all, stage_sizes, depth_count, group_count * src_count, row_total
    )
    depth_index = lax.axis_index("depth")
    flattened = lax.dynamic_slice_in_dim(sketch_all, depth_index * slab_width, slab_width, 1)
    local_planes = 1
    lower_factor = jnp.linalg.cholesky(gram_matrix)
    sketch_basis = lax.linalg.triangular_solve(
        lower_factor, flattened, left_side=True, lower=True
    ).reshape(probe_count, local_planes, slab_width)
    return (sketch_basis, lower_factor.T)


def solution(mesh):
    src_size, depth_size = mesh.devices.shape
    cut = mesh.devices.reshape(CHIPS_Y, CHIPS_Z, CORES, depth_size)
    fine = Mesh(cut, SRC_AXES + ("depth",))
    in_specs = (
        P(SRC_AXES, None, None, None),
        P(SRC_AXES),
        P(SRC_AXES),
        P(),
        P("depth", None),
        P(None, "depth", None),
    )
    out_specs = (P(None, "depth", SRC_AXES), P())
    return jax.shard_map(shards, mesh=fine, in_specs=in_specs, out_specs=out_specs, check_vma=False)
```

```python
import math

import jax
import jax.numpy as jnp
from jax import lax
from jax.experimental import pallas as pl
from jax.experimental.pallas import tpu as pltpu
from jax.sharding import Mesh, PartitionSpec as P

SIDE = 64
CHIPS_Y = 8
CHIPS_Z = 8
CORES = 2
SRC_AXES = ("chip_y", "chip_z", "core")


DAMPING = 0.5
STEP_DEPTH = 1.0


def dft_tables(points, direction):
    counter = jnp.arange(points, dtype=jnp.int32)
    product = counter[:, None] * counter[None, :] % points
    angles = 2.0 * math.pi / points * product.astype(jnp.float32)
    cosine = jnp.cos(angles) / math.sqrt(points)
    sine_part = direction * jnp.sin(angles) / math.sqrt(points)
    matrix = jnp.stack(
        [jnp.stack([cosine, sine_part], axis=1), jnp.stack([-sine_part, cosine], axis=1)], axis=0
    )
    matrix = matrix.astype(jnp.bfloat16)
    total_points = points * points
    twist_index = counter[:, None] * counter[None, :] % total_points
    twist_angle = 2.0 * math.pi / total_points * twist_index.astype(jnp.float32)
    return (matrix, jnp.cos(twist_angle), direction * jnp.sin(twist_angle))


def transform(values, tables):
    matrix, twist_real, twist_imag = tables
    points = matrix.shape[1]
    leading = values.shape[:-3]
    grid_values = values.reshape((-1, 2, points, points))
    segmented = jnp.einsum(
        "nrab,rasc->nscb", grid_values, matrix, preferred_element_type=jnp.float32
    )
    real_part = segmented[:, 0]
    imag_part = segmented[:, 1]
    turned = jnp.stack(
        [
            real_part * twist_real - imag_part * twist_imag,
            real_part * twist_imag + imag_part * twist_real,
        ],
        axis=1,
    ).astype(jnp.bfloat16)
    result = jnp.einsum("nscb,sbtd->ntdc", turned, matrix, preferred_element_type=jnp.float32)
    return result.reshape(leading + (2, points, points))


def complex_times(first, second):
    real_part = first[..., 0, :, :] * second[..., 0, :, :] - first[..., 1, :, :] * second[..., 1, :, :]
    imag_part = first[..., 0, :, :] * second[..., 1, :, :] + first[..., 1, :, :] * second[..., 0, :, :]
    return jnp.stack([real_part, imag_part], axis=-3)


def conjugate(values):
    return jnp.stack([values[..., 0, :, :], -values[..., 1, :, :]], axis=-3)


def propagate(values, spectrum, forward, inverse):
    moved_on = transform(values.astype(jnp.bfloat16), forward)
    return transform(complex_times(moved_on, spectrum).astype(jnp.bfloat16), inverse)


def propagator(wave_nums, points_all):
    counter = jnp.arange(points_all, dtype=jnp.int32)
    folded = jnp.where(counter < points_all // 2, counter, counter - points_all).astype(jnp.float32)
    lateral = 2.0 * math.pi / points_all * folded
    excess = wave_nums[:, None] ** 2 - lateral[None, :] ** 2
    upward = jnp.sqrt(jnp.maximum(excess, 0.0)) * STEP_DEPTH
    damped = jnp.sqrt(jnp.maximum(-excess, 0.0)) * STEP_DEPTH
    real_part = jnp.where(excess > 0, jnp.cos(upward), jnp.exp(-damped))
    imag_part = jnp.where(excess > 0, jnp.sin(upward), jnp.zeros_like(upward))
    return jnp.stack([real_part, imag_part], axis=1)


def screens(wave_nums, slowness):
    phase = wave_nums[:, None, None] * STEP_DEPTH * slowness[None]
    return jnp.stack([jnp.cos(phase), jnp.sin(phase)], axis=2)


def encoded_sources(incident, encode, sources):
    shifts = jnp.arange(sources, dtype=jnp.int32)
    bit_set = encode[:, None] >> shifts[None, :] & 1
    signs_all = (1 - 2 * bit_set).astype(jnp.float32)
    return jnp.sum(signs_all[:, :, None, None] * incident, axis=1)


def lookup_waves(freq_index, wavenum, table_size):
    onehot_rows = (freq_index[:, None] == jnp.arange(table_size, dtype=jnp.int32)[None, :]).astype(
        jnp.float32
    )
    return jnp.sum(onehot_rows * wavenum[None, :], axis=1)


def member_of(group):
    index = 0
    total = 1
    for axis, size in group:
        index = index * size + lax.axis_index(axis)
        total *= size
    return index, total


def device_of(group, index):
    place = {}
    for axis, size in reversed(group):
        place[axis] = lax.rem(index, size)
        index = index // size
    return place


def exchange(group, current, slot, send_sems, recv_sems, offset, whole=False):
    me, size = member_of(group)
    copies = []
    for step in range(1, size):
        peer = lax.rem(me + step, size)
        copy = pltpu.make_async_remote_copy(
            src_ref=current if whole else current.at[peer],
            dst_ref=slot.at[me],
            send_sem=send_sems.at[offset + peer],
            recv_sem=recv_sems.at[offset + me],
            device_id=device_of(group, peer),
            device_id_type=pl.DeviceIdType.MESH,
        )
        copy.start()
        copies.append(copy)
    for copy in copies:
        copy.wait_send()
    for step in range(1, size):
        sender = lax.rem(me + size - step, size)
        incoming = pltpu.make_async_remote_copy(
            src_ref=current if whole else current.at[sender],
            dst_ref=slot.at[sender],
            send_sem=send_sems.at[offset + sender],
            recv_sem=recv_sems.at[offset + sender],
            device_id=device_of(group, sender),
            device_id_type=pl.DeviceIdType.MESH,
        )
        incoming.wait_recv()
    return me


def reduce_kernel(stages, gram_groups, depth_size, divisor, row_total, part_ref, probe_ref, sketch_ref,
                  gram_ref, *scratch):
    count = len(stages)
    slots = scratch[:count]
    sums = scratch[count : 2 * count - 1]
    groups = len(gram_groups)
    gram_slots = scratch[2 * count - 1 : 2 * count - 1 + groups]
    mine, gathered, carried, send_sems, recv_sems = scratch[2 * count - 1 + groups :]
    barrier = pltpu.get_barrier_semaphore()
    peers_total = 0
    for group in gram_groups + [[("depth", depth_size)]]:
        me, size = member_of(group)
        for step in range(1, size):
            pl.semaphore_signal(barrier, inc=1, device_id=device_of(group, lax.rem(me + step, size)),
                                device_id_type=pl.DeviceIdType.MESH)
            peers_total += 1
    pl.semaphore_wait(barrier, peers_total)
    current = part_ref
    offset = 0
    for stage, (axis, size) in enumerate(stages):
        me = exchange([(axis, size)], current, slots[stage], send_sems, recv_sems, offset)
        offset += size
        total = current[me]
        for step in range(1, size):
            total = total + slots[stage][lax.rem(me + size - step, size)]
        if stage + 1 < count:
            sums[stage][...] = total
            current = sums[stage]
        else:
            mine[...] = total
    me = exchange([("depth", depth_size)], mine, gathered, send_sems, recv_sems, offset, whole=True)
    offset += depth_size
    gathered[me] = mine[...]
    summed = gathered[...].reshape(sketch_ref.shape)
    sketch = summed / divisor + DAMPING * probe_ref[...]
    sketch_ref[...] = sketch
    carried[...] = lax.dot_general(
        sketch, sketch, (((1,), (1,)), ((), ())), precision=lax.Precision.HIGHEST,
        preferred_element_type=jnp.float32,
    ) / row_total
    for stage, group in enumerate(gram_groups):
        slot = gram_slots[stage]
        size = member_of(group)[1]
        me = exchange(group, carried, slot, send_sems, recv_sems, offset, whole=True)
        offset += size
        slot[me] = carried[...]
        total = slot[0]
        for member in range(1, size):
            total = total + slot[member]
        carried[...] = total
    gram_ref[...] = carried[...]


def reduce_all(part, probe_all, stages, depth_size, divisor, row_total):
    stages = [(axis, size) for axis, size in stages if size > 1]
    part = part.reshape(tuple(size for _, size in stages) + part.shape[-2:])
    rows, width = probe_all.shape
    scratch = [pltpu.VMEM(part.shape[stage:], jnp.float32) for stage in range(len(stages))]
    scratch += [pltpu.VMEM(part.shape[stage + 1 :], jnp.float32) for stage in range(len(stages) - 1)]
    gram_groups = [stages[:2]] + [[stage] for stage in stages[2:]]
    group_sizes = [math.prod(size for _, size in group) for group in gram_groups]
    scratch += [pltpu.VMEM((size, rows, rows), jnp.float32) for size in group_sizes]
    semaphores = sum(size for _, size in stages) + depth_size + sum(group_sizes)
    scratch += [
        pltpu.VMEM(part.shape[-2:], jnp.float32),
        pltpu.VMEM((depth_size,) + part.shape[-2:], jnp.float32),
        pltpu.VMEM((rows, rows), jnp.float32),
        pltpu.SemaphoreType.DMA((semaphores,)),
        pltpu.SemaphoreType.DMA((semaphores,)),
    ]
    return pl.pallas_call(
        lambda *refs: reduce_kernel(stages, gram_groups, depth_size, divisor, row_total, *refs),
        out_shape=(
            jax.ShapeDtypeStruct((rows, width), jnp.float32),
            jax.ShapeDtypeStruct((rows, rows), jnp.float32),
        ),
        in_specs=[pl.BlockSpec(memory_space=pltpu.VMEM)] * 2,
        out_specs=(pl.BlockSpec(memory_space=pltpu.VMEM), pl.BlockSpec(memory_space=pltpu.VMEM)),
        scratch_shapes=scratch,
        compiler_params=pltpu.CompilerParams(collective_id=2, has_side_effects=True),
    )(part, probe_all)


def shards(incident, encode, freq_index, wavenum, slowness, probes):
    points_all = SIDE * SIDE
    forward = dft_tables(SIDE, -1.0)
    inverse = dft_tables(SIDE, 1.0)
    group_count = incident.shape[0]
    probe_count = probes.shape[0]
    src_count = lax.axis_size(SRC_AXES)
    depth_count = lax.axis_size("depth")
    rows = probe_count // depth_count
    points = probes.shape[2]
    slab_points = points // src_count
    probe_slab = lax.dynamic_slice_in_dim(
        probes, lax.axis_index(SRC_AXES) * slab_points, slab_points, 2
    )
    high = slowness.astype(jnp.bfloat16)
    rest = slowness - high.astype(jnp.float32)
    middle = rest.astype(jnp.bfloat16)
    low = (rest - middle.astype(jnp.float32)).astype(jnp.bfloat16)
    shared = jnp.concatenate([probe_slab.reshape(-1), high.reshape(-1), middle.reshape(-1), low.reshape(-1)])
    payload = jnp.concatenate(
        [probes.reshape(depth_count, -1), jnp.broadcast_to(shared[None], (depth_count,) + shared.shape)],
        axis=1,
    )
    payload = lax.all_to_all(payload, "depth", 0, 0, tiled=True)
    cut = rows * points
    probe_mine = jnp.transpose(payload[:, :cut].reshape(depth_count, rows, points), (1, 0, 2))
    probe_mine = probe_mine.astype(jnp.float32)
    probe_mine = probe_mine.reshape(probe_mine.shape[:2] + (SIDE, SIDE))
    slab_size = probe_count * slab_points
    probe_all = payload[:, cut : cut + slab_size].reshape(depth_count, probe_count, slab_points)
    probe_all = jnp.transpose(probe_all, (1, 0, 2)).reshape(probe_count, -1).astype(jnp.float32)
    parts = payload[:, cut + slab_size :].reshape(depth_count, 3, points).astype(jnp.float32)
    slowness_all = (parts[:, 0] + parts[:, 1]) + parts[:, 2]
    plane_count = slowness_all.shape[0]
    sources = encoded_sources(incident, encode, incident.shape[1])
    sources = sources.reshape(sources.shape[:-1] + (SIDE, SIDE))
    wave_nums = lookup_waves(freq_index, wavenum, wavenum.shape[0])
    spectra = propagator(wave_nums, points_all)
    spectra = spectra.reshape(spectra.shape[:-1] + (SIDE, SIDE))
    spectra_back = conjugate(spectra)
    plane_screens = screens(wave_nums, slowness_all)
    plane_screens = plane_screens.reshape(plane_screens.shape[:-1] + (SIDE, SIDE))
    born_scale = wave_nums * STEP_DEPTH

    fields = []
    current = sources
    for plane in range(plane_count):
        current = complex_times(plane_screens[:, plane], propagate(current, spectra, forward, inverse))
        fields.append(current)

    def born(plane):
        scaled = born_scale[:, None, None, None] * probe_mine[None, :, plane]
        background = fields[plane]
        return jnp.stack([-scaled * background[:, None, 1], scaled * background[:, None, 0]], axis=2)

    tangent = born(0)
    for plane in range(1, plane_count):
        moved_on = complex_times(
            plane_screens[:, plane][:, None], propagate(tangent, spectra[:, None], forward, inverse)
        )
        tangent = moved_on + born(plane)

    adjoint = tangent
    pieces = [None] * plane_count
    for plane in reversed(range(plane_count)):
        background = fields[plane]
        product_terms = born_scale[:, None, None, None] * (
            background[:, None, 0] * adjoint[:, :, 1] - background[:, None, 1] * adjoint[:, :, 0]
        )
        pieces[plane] = jnp.sum(product_terms, axis=0)
        if plane > 0:
            turned_back = complex_times(conjugate(plane_screens[:, plane])[:, None], adjoint)
            adjoint = propagate(turned_back, spectra_back[:, None], forward, inverse)
    sketch_part = lax.optimization_barrier(jnp.stack(pieces, axis=1))
    rows, planes = sketch_part.shape[0], sketch_part.shape[1]
    by_axes = sketch_part.reshape(rows, planes, CHIPS_Y, CHIPS_Z, CORES, -1)
    slab_width = by_axes.shape[-1]
    by_axes = jnp.transpose(by_axes, (4, 3, 2, 0, 1, 5)).reshape(
        CORES, CHIPS_Z, CHIPS_Y, rows, planes * slab_width
    )
    stage_sizes = [("core", CORES), ("chip_z", CHIPS_Z), ("chip_y", CHIPS_Y)]
    row_total = planes * slab_width * src_count
    sketch_all, gram_matrix = reduce_all(
        by_axes, probe_all, stage_sizes, depth_count, group_count * src_count, row_total
    )
    depth_index = lax.axis_index("depth")
    flattened = lax.dynamic_slice_in_dim(sketch_all, depth_index * slab_width, slab_width, 1)
    local_planes = 1
    lower_factor = jnp.linalg.cholesky(gram_matrix)
    sketch_basis = lax.linalg.triangular_solve(
        lower_factor, flattened, left_side=True, lower=True
    ).reshape(probe_count, local_planes, slab_width)
    return (sketch_basis, lower_factor.T)


def solution(mesh):
    src_size, depth_size = mesh.devices.shape
    cut = mesh.devices.reshape(CHIPS_Y, CHIPS_Z, CORES, depth_size)
    fine = Mesh(cut, SRC_AXES + ("depth",))
    in_specs = (
        P(SRC_AXES, None, None, None),
        P(SRC_AXES),
        P(SRC_AXES),
        P(),
        P("depth", None),
        P(None, "depth", None),
    )
    out_specs = (P(None, "depth", SRC_AXES), P())
    return jax.shard_map(shards, mesh=fine, in_specs=in_specs, out_specs=out_specs, check_vma=False)
```

```python
import math

import jax
import jax.numpy as jnp
from jax import lax
from jax.experimental import pallas as pl
from jax.experimental.pallas import tpu as pltpu
from jax.sharding import Mesh, PartitionSpec as P

SIDE = 64
CHIPS_Y = 8
CHIPS_Z = 8
CORES = 2
SRC_AXES = ("chip_y", "chip_z", "core")


DAMPING = 0.5
STEP_DEPTH = 1.0


def dft_tables(points, direction):
    counter = jnp.arange(points, dtype=jnp.int32)
    product = counter[:, None] * counter[None, :] % points
    angles = 2.0 * math.pi / points * product.astype(jnp.float32)
    cosine = jnp.cos(angles) / math.sqrt(points)
    sine_part = direction * jnp.sin(angles) / math.sqrt(points)
    matrix = jnp.stack(
        [jnp.stack([cosine, sine_part], axis=1), jnp.stack([-sine_part, cosine], axis=1)], axis=0
    )
    matrix = matrix.astype(jnp.bfloat16)
    total_points = points * points
    twist_index = counter[:, None] * counter[None, :] % total_points
    twist_angle = 2.0 * math.pi / total_points * twist_index.astype(jnp.float32)
    return (matrix, jnp.cos(twist_angle), direction * jnp.sin(twist_angle))


def transform(values, tables):
    matrix, twist_real, twist_imag = tables
    points = matrix.shape[1]
    leading = values.shape[:-3]
    grid_values = values.reshape((-1, 2, points, points))
    segmented = jnp.einsum(
        "nrab,rasc->nscb", grid_values, matrix, preferred_element_type=jnp.float32
    )
    real_part = segmented[:, 0]
    imag_part = segmented[:, 1]
    turned = jnp.stack(
        [
            real_part * twist_real - imag_part * twist_imag,
            real_part * twist_imag + imag_part * twist_real,
        ],
        axis=1,
    ).astype(jnp.bfloat16)
    result = jnp.einsum("nscb,sbtd->ntdc", turned, matrix, preferred_element_type=jnp.float32)
    return result.reshape(leading + (2, points, points))


def complex_times(first, second):
    real_part = first[..., 0, :, :] * second[..., 0, :, :] - first[..., 1, :, :] * second[..., 1, :, :]
    imag_part = first[..., 0, :, :] * second[..., 1, :, :] + first[..., 1, :, :] * second[..., 0, :, :]
    return jnp.stack([real_part, imag_part], axis=-3)


def conjugate(values):
    return jnp.stack([values[..., 0, :, :], -values[..., 1, :, :]], axis=-3)


def propagate(values, spectrum, forward, inverse):
    moved_on = transform(values.astype(jnp.bfloat16), forward)
    return transform(complex_times(moved_on, spectrum).astype(jnp.bfloat16), inverse)


def propagator(wave_nums, points_all):
    counter = jnp.arange(points_all, dtype=jnp.int32)
    folded = jnp.where(counter < points_all // 2, counter, counter - points_all).astype(jnp.float32)
    lateral = 2.0 * math.pi / points_all * folded
    excess = wave_nums[:, None] ** 2 - lateral[None, :] ** 2
    upward = jnp.sqrt(jnp.maximum(excess, 0.0)) * STEP_DEPTH
    damped = jnp.sqrt(jnp.maximum(-excess, 0.0)) * STEP_DEPTH
    real_part = jnp.where(excess > 0, jnp.cos(upward), jnp.exp(-damped))
    imag_part = jnp.where(excess > 0, jnp.sin(upward), jnp.zeros_like(upward))
    return jnp.stack([real_part, imag_part], axis=1)


def screens(wave_nums, slowness):
    phase = wave_nums[:, None, None] * STEP_DEPTH * slowness[None]
    return jnp.stack([jnp.cos(phase), jnp.sin(phase)], axis=2)


def encoded_sources(incident, encode, sources):
    shifts = jnp.arange(sources, dtype=jnp.int32)
    bit_set = encode[:, None] >> shifts[None, :] & 1
    signs_all = (1 - 2 * bit_set).astype(jnp.float32)
    return jnp.sum(signs_all[:, :, None, None] * incident, axis=1)


def lookup_waves(freq_index, wavenum, table_size):
    onehot_rows = (freq_index[:, None] == jnp.arange(table_size, dtype=jnp.int32)[None, :]).astype(
        jnp.float32
    )
    return jnp.sum(onehot_rows * wavenum[None, :], axis=1)


def exchange(axis, size, current, slot, send_sems, recv_sems, offset, whole=False):
    me = lax.axis_index(axis)
    copies = []
    for step in range(1, size):
        peer = lax.rem(me + step, size)
        copy = pltpu.make_async_remote_copy(
            src_ref=current if whole else current.at[peer],
            dst_ref=slot.at[me],
            send_sem=send_sems.at[offset + peer],
            recv_sem=recv_sems.at[offset + me],
            device_id={axis: peer},
            device_id_type=pl.DeviceIdType.MESH,
        )
        copy.start()
        copies.append(copy)
    for copy in copies:
        copy.wait_send()
    for step in range(1, size):
        sender = lax.rem(me + size - step, size)
        incoming = pltpu.make_async_remote_copy(
            src_ref=current if whole else current.at[sender],
            dst_ref=slot.at[sender],
            send_sem=send_sems.at[offset + sender],
            recv_sem=recv_sems.at[offset + sender],
            device_id={axis: sender},
            device_id_type=pl.DeviceIdType.MESH,
        )
        incoming.wait_recv()
    return me


def reduce_kernel(stages, depth_size, divisor, row_total, part_ref, probe_ref, sketch_ref, gram_ref,
                  *scratch):
    count = len(stages)
    slots = scratch[:count]
    sums = scratch[count : 2 * count - 1]
    gram_slots = scratch[2 * count - 1 : 3 * count - 1]
    mine, gathered, carried, send_sems, recv_sems = scratch[3 * count - 1 :]
    barrier = pltpu.get_barrier_semaphore()
    peers_total = 0
    for axis, size in stages + [("depth", depth_size)]:
        me = lax.axis_index(axis)
        for step in range(1, size):
            pl.semaphore_signal(barrier, inc=1, device_id={axis: lax.rem(me + step, size)},
                                device_id_type=pl.DeviceIdType.MESH)
            peers_total += 1
    pl.semaphore_wait(barrier, peers_total)
    current = part_ref
    offset = 0
    for stage, (axis, size) in enumerate(stages):
        me = exchange(axis, size, current, slots[stage], send_sems, recv_sems, offset)
        offset += size
        total = current[me]
        for step in range(1, size):
            total = total + slots[stage][lax.rem(me + size - step, size)]
        if stage + 1 < count:
            sums[stage][...] = total
            current = sums[stage]
        else:
            mine[...] = total
    me = exchange("depth", depth_size, mine, gathered, send_sems, recv_sems, offset, whole=True)
    offset += depth_size
    gathered[me] = mine[...]
    summed = gathered[...].reshape(sketch_ref.shape)
    sketch = summed / divisor + DAMPING * probe_ref[...]
    sketch_ref[...] = sketch
    carried[...] = lax.dot_general(
        sketch, sketch, (((1,), (1,)), ((), ())), precision=lax.Precision.HIGHEST,
        preferred_element_type=jnp.float32,
    ) / row_total
    for stage, (axis, size) in enumerate(stages):
        slot = gram_slots[stage]
        me = exchange(axis, size, carried, slot, send_sems, recv_sems, offset, whole=True)
        offset += size
        slot[me] = carried[...]
        total = slot[0]
        for member in range(1, size):
            total = total + slot[member]
        carried[...] = total
    gram_ref[...] = carried[...]


def reduce_all(part, probe_all, stages, depth_size, divisor, row_total):
    stages = [(axis, size) for axis, size in stages if size > 1]
    part = part.reshape(tuple(size for _, size in stages) + part.shape[-2:])
    rows, width = probe_all.shape
    scratch = [pltpu.VMEM(part.shape[stage:], jnp.float32) for stage in range(len(stages))]
    scratch += [pltpu.VMEM(part.shape[stage + 1 :], jnp.float32) for stage in range(len(stages) - 1)]
    scratch += [pltpu.VMEM((size, rows, rows), jnp.float32) for _, size in stages]
    semaphores = 2 * sum(size for _, size in stages) + depth_size
    scratch += [
        pltpu.VMEM(part.shape[-2:], jnp.float32),
        pltpu.VMEM((depth_size,) + part.shape[-2:], jnp.float32),
        pltpu.VMEM((rows, rows), jnp.float32),
        pltpu.SemaphoreType.DMA((semaphores,)),
        pltpu.SemaphoreType.DMA((semaphores,)),
    ]
    return pl.pallas_call(
        lambda *refs: reduce_kernel(stages, depth_size, divisor, row_total, *refs),
        out_shape=(
            jax.ShapeDtypeStruct((rows, width), jnp.float32),
            jax.ShapeDtypeStruct((rows, rows), jnp.float32),
        ),
        in_specs=[pl.BlockSpec(memory_space=pltpu.VMEM)] * 2,
        out_specs=(pl.BlockSpec(memory_space=pltpu.VMEM), pl.BlockSpec(memory_space=pltpu.VMEM)),
        scratch_shapes=scratch,
        compiler_params=pltpu.CompilerParams(collective_id=2, has_side_effects=True),
    )(part, probe_all)


def shards(incident, encode, freq_index, wavenum, slowness, probes):
    points_all = SIDE * SIDE
    forward = dft_tables(SIDE, -1.0)
    inverse = dft_tables(SIDE, 1.0)
    group_count = incident.shape[0]
    probe_count = probes.shape[0]
    src_count = lax.axis_size(SRC_AXES)
    depth_count = lax.axis_size("depth")
    rows = probe_count // depth_count
    points = probes.shape[2]
    slab_points = points // src_count
    probe_slab = lax.dynamic_slice_in_dim(
        probes, lax.axis_index(SRC_AXES) * slab_points, slab_points, 2
    )
    high = slowness.astype(jnp.bfloat16)
    rest = slowness - high.astype(jnp.float32)
    middle = rest.astype(jnp.bfloat16)
    low = (rest - middle.astype(jnp.float32)).astype(jnp.bfloat16)
    shared = jnp.concatenate([probe_slab.reshape(-1), high.reshape(-1), middle.reshape(-1), low.reshape(-1)])
    payload = jnp.concatenate(
        [probes.reshape(depth_count, -1), jnp.broadcast_to(shared[None], (depth_count,) + shared.shape)],
        axis=1,
    )
    payload = lax.all_to_all(payload, "depth", 0, 0, tiled=True)
    cut = rows * points
    probe_mine = jnp.transpose(payload[:, :cut].reshape(depth_count, rows, points), (1, 0, 2))
    probe_mine = probe_mine.astype(jnp.float32)
    probe_mine = probe_mine.reshape(probe_mine.shape[:2] + (SIDE, SIDE))
    slab_size = probe_count * slab_points
    probe_all = payload[:, cut : cut + slab_size].reshape(depth_count, probe_count, slab_points)
    probe_all = jnp.transpose(probe_all, (1, 0, 2)).reshape(probe_count, -1).astype(jnp.float32)
    parts = payload[:, cut + slab_size :].reshape(depth_count, 3, points).astype(jnp.float32)
    slowness_all = (parts[:, 0] + parts[:, 1]) + parts[:, 2]
    plane_count = slowness_all.shape[0]
    sources = encoded_sources(incident, encode, incident.shape[1])
    sources = sources.reshape(sources.shape[:-1] + (SIDE, SIDE))
    wave_nums = lookup_waves(freq_index, wavenum, wavenum.shape[0])
    spectra = propagator(wave_nums, points_all)
    spectra = spectra.reshape(spectra.shape[:-1] + (SIDE, SIDE))
    spectra_back = conjugate(spectra)
    plane_screens = screens(wave_nums, slowness_all)
    plane_screens = plane_screens.reshape(plane_screens.shape[:-1] + (SIDE, SIDE))
    born_scale = wave_nums * STEP_DEPTH

    fields = [complex_times(plane_screens[:, 0], propagate(sources, spectra, forward, inverse))]

    def born(plane):
        scaled = born_scale[:, None, None, None] * probe_mine[None, :, plane]
        background = fields[plane]
        return jnp.stack([-scaled * background[:, None, 1], scaled * background[:, None, 0]], axis=2)

    tangent = born(0)
    for plane in range(1, plane_count):
        both = jnp.concatenate([fields[-1][:, None], tangent], axis=1)
        moved_on = complex_times(
            plane_screens[:, plane][:, None], propagate(both, spectra[:, None], forward, inverse)
        )
        fields.append(moved_on[:, 0])
        tangent = moved_on[:, 1:] + born(plane)

    adjoint = tangent
    pieces = [None] * plane_count
    for plane in reversed(range(plane_count)):
        background = fields[plane]
        product_terms = born_scale[:, None, None, None] * (
            background[:, None, 0] * adjoint[:, :, 1] - background[:, None, 1] * adjoint[:, :, 0]
        )
        pieces[plane] = jnp.sum(product_terms, axis=0)
        if plane > 0:
            turned_back = complex_times(conjugate(plane_screens[:, plane])[:, None], adjoint)
            adjoint = propagate(turned_back, spectra_back[:, None], forward, inverse)
    sketch_part = lax.optimization_barrier(jnp.stack(pieces, axis=1))
    rows, planes = sketch_part.shape[0], sketch_part.shape[1]
    by_axes = sketch_part.reshape(rows, planes, CHIPS_Y, CHIPS_Z, CORES, -1)
    slab_width = by_axes.shape[-1]
    by_axes = jnp.transpose(by_axes, (4, 3, 2, 0, 1, 5)).reshape(
        CORES, CHIPS_Z, CHIPS_Y, rows, planes * slab_width
    )
    stage_sizes = [("core", CORES), ("chip_z", CHIPS_Z), ("chip_y", CHIPS_Y)]
    row_total = planes * slab_width * src_count
    sketch_all, gram_matrix = reduce_all(
        by_axes, probe_all, stage_sizes, depth_count, group_count * src_count, row_total
    )
    depth_index = lax.axis_index("depth")
    flattened = lax.dynamic_slice_in_dim(sketch_all, depth_index * slab_width, slab_width, 1)
    local_planes = 1
    lower_factor = jnp.linalg.cholesky(gram_matrix)
    sketch_basis = lax.linalg.triangular_solve(
        lower_factor, flattened, left_side=True, lower=True
    ).reshape(probe_count, local_planes, slab_width)
    return (sketch_basis, lower_factor.T)


def solution(mesh):
    src_size, depth_size = mesh.devices.shape
    cut = mesh.devices.reshape(CHIPS_Y, CHIPS_Z, CORES, depth_size)
    fine = Mesh(cut, SRC_AXES + ("depth",))
    in_specs = (
        P(SRC_AXES, None, None, None),
        P(SRC_AXES),
        P(SRC_AXES),
        P(),
        P("depth", None),
        P(None, "depth", None),
    )
    out_specs = (P(None, "depth", SRC_AXES), P())
    return jax.shard_map(shards, mesh=fine, in_specs=in_specs, out_specs=out_specs, check_vma=False)
```

```python
import math

import jax
import jax.numpy as jnp
from jax import lax
from jax.experimental import pallas as pl
from jax.experimental.pallas import tpu as pltpu
from jax.sharding import Mesh, PartitionSpec as P

SIDE = 64
CHIPS_Y = 8
CHIPS_Z = 8
CORES = 2
SRC_AXES = ("chip_y", "chip_z", "core")


DAMPING = 0.5
STEP_DEPTH = 1.0


def dft_tables(points, direction):
    counter = jnp.arange(points, dtype=jnp.int32)
    product = counter[:, None] * counter[None, :] % points
    angles = 2.0 * math.pi / points * product.astype(jnp.float32)
    cosine = jnp.cos(angles) / math.sqrt(points)
    sine_part = direction * jnp.sin(angles) / math.sqrt(points)
    matrix = jnp.stack(
        [jnp.stack([cosine, sine_part], axis=1), jnp.stack([-sine_part, cosine], axis=1)], axis=0
    )
    matrix = matrix.astype(jnp.bfloat16)
    total_points = points * points
    twist_index = counter[:, None] * counter[None, :] % total_points
    twist_angle = 2.0 * math.pi / total_points * twist_index.astype(jnp.float32)
    return (matrix, jnp.cos(twist_angle), direction * jnp.sin(twist_angle))


def transform(values, tables):
    matrix, twist_real, twist_imag = tables
    points = matrix.shape[1]
    leading = values.shape[:-3]
    grid_values = values.reshape((-1, 2, points, points))
    segmented = jnp.einsum(
        "nrab,rasc->nscb", grid_values, matrix, preferred_element_type=jnp.float32
    )
    real_part = segmented[:, 0]
    imag_part = segmented[:, 1]
    turned = jnp.stack(
        [
            real_part * twist_real - imag_part * twist_imag,
            real_part * twist_imag + imag_part * twist_real,
        ],
        axis=1,
    ).astype(jnp.bfloat16)
    result = jnp.einsum("nscb,sbtd->ntdc", turned, matrix, preferred_element_type=jnp.float32)
    return result.reshape(leading + (2, points, points))


def complex_times(first, second):
    real_part = first[..., 0, :, :] * second[..., 0, :, :] - first[..., 1, :, :] * second[..., 1, :, :]
    imag_part = first[..., 0, :, :] * second[..., 1, :, :] + first[..., 1, :, :] * second[..., 0, :, :]
    return jnp.stack([real_part, imag_part], axis=-3)


def conjugate(values):
    return jnp.stack([values[..., 0, :, :], -values[..., 1, :, :]], axis=-3)


def propagate(values, spectrum, forward, inverse):
    moved_on = transform(values.astype(jnp.bfloat16), forward)
    return transform(complex_times(moved_on, spectrum).astype(jnp.bfloat16), inverse)


def propagator(wave_nums, points_all):
    counter = jnp.arange(points_all, dtype=jnp.int32)
    folded = jnp.where(counter < points_all // 2, counter, counter - points_all).astype(jnp.float32)
    lateral = 2.0 * math.pi / points_all * folded
    excess = wave_nums[:, None] ** 2 - lateral[None, :] ** 2
    upward = jnp.sqrt(jnp.maximum(excess, 0.0)) * STEP_DEPTH
    damped = jnp.sqrt(jnp.maximum(-excess, 0.0)) * STEP_DEPTH
    real_part = jnp.where(excess > 0, jnp.cos(upward), jnp.exp(-damped))
    imag_part = jnp.where(excess > 0, jnp.sin(upward), jnp.zeros_like(upward))
    return jnp.stack([real_part, imag_part], axis=1)


def screens(wave_nums, slowness):
    phase = wave_nums[:, None, None] * STEP_DEPTH * slowness[None]
    return jnp.stack([jnp.cos(phase), jnp.sin(phase)], axis=2)


def encoded_sources(incident, encode, sources):
    shifts = jnp.arange(sources, dtype=jnp.int32)
    bit_set = encode[:, None] >> shifts[None, :] & 1
    signs_all = (1 - 2 * bit_set).astype(jnp.float32)
    return jnp.sum(signs_all[:, :, None, None] * incident, axis=1)


def lookup_waves(freq_index, wavenum, table_size):
    onehot_rows = (freq_index[:, None] == jnp.arange(table_size, dtype=jnp.int32)[None, :]).astype(
        jnp.float32
    )
    return jnp.sum(onehot_rows * wavenum[None, :], axis=1)


def exchange(axis, size, current, slot, send_sems, recv_sems, offset, whole=False):
    me = lax.axis_index(axis)
    copies = []
    for step in range(1, size):
        peer = lax.rem(me + step, size)
        copy = pltpu.make_async_remote_copy(
            src_ref=current if whole else current.at[peer],
            dst_ref=slot.at[me],
            send_sem=send_sems.at[offset + peer],
            recv_sem=recv_sems.at[offset + me],
            device_id={axis: peer},
            device_id_type=pl.DeviceIdType.MESH,
        )
        copy.start()
        copies.append(copy)
    for copy in copies:
        copy.wait_send()
    for step in range(1, size):
        sender = lax.rem(me + size - step, size)
        incoming = pltpu.make_async_remote_copy(
            src_ref=current if whole else current.at[sender],
            dst_ref=slot.at[sender],
            send_sem=send_sems.at[offset + sender],
            recv_sem=recv_sems.at[offset + sender],
            device_id={axis: sender},
            device_id_type=pl.DeviceIdType.MESH,
        )
        incoming.wait_recv()
    return me


def reduce_kernel(stages, depth_size, divisor, row_total, part_ref, probe_ref, sketch_ref, gram_ref,
                  *scratch):
    count = len(stages)
    slots = scratch[:count]
    sums = scratch[count : 2 * count - 1]
    gram_slots = scratch[2 * count - 1 : 3 * count - 1]
    mine, gathered, carried, send_sems, recv_sems = scratch[3 * count - 1 :]
    barrier = pltpu.get_barrier_semaphore()
    peers_total = 0
    for axis, size in stages + [("depth", depth_size)]:
        me = lax.axis_index(axis)
        for step in range(1, size):
            pl.semaphore_signal(barrier, inc=1, device_id={axis: lax.rem(me + step, size)},
                                device_id_type=pl.DeviceIdType.MESH)
            peers_total += 1
    pl.semaphore_wait(barrier, peers_total)
    current = part_ref
    offset = 0
    for stage, (axis, size) in enumerate(stages):
        me = exchange(axis, size, current, slots[stage], send_sems, recv_sems, offset)
        offset += size
        total = current[me]
        for step in range(1, size):
            total = total + slots[stage][lax.rem(me + size - step, size)]
        if stage + 1 < count:
            sums[stage][...] = total
            current = sums[stage]
        else:
            mine[...] = total
    me = exchange("depth", depth_size, mine, gathered, send_sems, recv_sems, offset, whole=True)
    offset += depth_size
    gathered[me] = mine[...]
    summed = gathered[...].reshape(sketch_ref.shape)
    sketch = summed / divisor + DAMPING * probe_ref[...]
    sketch_ref[...] = sketch
    carried[...] = lax.dot_general(
        sketch, sketch, (((1,), (1,)), ((), ())), precision=lax.Precision.HIGHEST,
        preferred_element_type=jnp.float32,
    ) / row_total
    for stage, (axis, size) in enumerate(stages):
        slot = gram_slots[stage]
        me = exchange(axis, size, carried, slot, send_sems, recv_sems, offset, whole=True)
        offset += size
        slot[me] = carried[...]
        total = slot[0]
        for member in range(1, size):
            total = total + slot[member]
        carried[...] = total
    gram_ref[...] = carried[...]


def reduce_all(part, probe_all, stages, depth_size, divisor, row_total):
    stages = [(axis, size) for axis, size in stages if size > 1]
    part = part.reshape(tuple(size for _, size in stages) + part.shape[-2:])
    rows, width = probe_all.shape
    scratch = [pltpu.VMEM(part.shape[stage:], jnp.float32) for stage in range(len(stages))]
    scratch += [pltpu.VMEM(part.shape[stage + 1 :], jnp.float32) for stage in range(len(stages) - 1)]
    scratch += [pltpu.VMEM((size, rows, rows), jnp.float32) for _, size in stages]
    semaphores = 2 * sum(size for _, size in stages) + depth_size
    scratch += [
        pltpu.VMEM(part.shape[-2:], jnp.float32),
        pltpu.VMEM((depth_size,) + part.shape[-2:], jnp.float32),
        pltpu.VMEM((rows, rows), jnp.float32),
        pltpu.SemaphoreType.DMA((semaphores,)),
        pltpu.SemaphoreType.DMA((semaphores,)),
    ]
    return pl.pallas_call(
        lambda *refs: reduce_kernel(stages, depth_size, divisor, row_total, *refs),
        out_shape=(
            jax.ShapeDtypeStruct((rows, width), jnp.float32),
            jax.ShapeDtypeStruct((rows, rows), jnp.float32),
        ),
        in_specs=[pl.BlockSpec(memory_space=pltpu.VMEM)] * 2,
        out_specs=(pl.BlockSpec(memory_space=pltpu.VMEM), pl.BlockSpec(memory_space=pltpu.VMEM)),
        scratch_shapes=scratch,
        compiler_params=pltpu.CompilerParams(collective_id=2, has_side_effects=True),
    )(part, probe_all)


def shards(incident, encode, freq_index, wavenum, slowness, probes):
    points_all = SIDE * SIDE
    forward = dft_tables(SIDE, -1.0)
    inverse = dft_tables(SIDE, 1.0)
    group_count = incident.shape[0]
    probe_count = probes.shape[0]
    src_count = lax.axis_size(SRC_AXES)
    depth_count = lax.axis_size("depth")
    rows = probe_count // depth_count
    points = probes.shape[2]
    slab_points = points // src_count
    probe_slab = lax.dynamic_slice_in_dim(
        probes, lax.axis_index(SRC_AXES) * slab_points, slab_points, 2
    )
    high = slowness.astype(jnp.bfloat16)
    rest = slowness - high.astype(jnp.float32)
    middle = rest.astype(jnp.bfloat16)
    low = (rest - middle.astype(jnp.float32)).astype(jnp.bfloat16)
    slab_size = probe_count * slab_points
    slab_rows = -(-slab_size // points)
    slab_row = jnp.pad(probe_slab.reshape(-1), (0, slab_rows * points - slab_size)).reshape(slab_rows, points)
    shared = jnp.concatenate([slab_row, high, middle, low], axis=0)
    payload = jnp.concatenate(
        [
            probes.reshape(depth_count, rows, points),
            jnp.broadcast_to(shared[None], (depth_count,) + shared.shape),
        ],
        axis=1,
    )
    payload = lax.all_to_all(payload, "depth", 0, 0, tiled=True)
    probe_mine = jnp.transpose(payload[:, :rows], (1, 0, 2)).astype(jnp.float32)
    probe_mine = probe_mine.reshape(probe_mine.shape[:2] + (SIDE, SIDE))
    probe_all = payload[:, rows : rows + slab_rows].reshape(depth_count, -1)[:, :slab_size]
    probe_all = probe_all.reshape(depth_count, probe_count, slab_points)
    probe_all = jnp.transpose(probe_all, (1, 0, 2)).reshape(probe_count, -1).astype(jnp.float32)
    parts = payload[:, rows + slab_rows :].astype(jnp.float32)
    slowness_all = (parts[:, 0] + parts[:, 1]) + parts[:, 2]
    plane_count = slowness_all.shape[0]
    sources = encoded_sources(incident, encode, incident.shape[1])
    sources = sources.reshape(sources.shape[:-1] + (SIDE, SIDE))
    wave_nums = lookup_waves(freq_index, wavenum, wavenum.shape[0])
    spectra = propagator(wave_nums, points_all)
    spectra = spectra.reshape(spectra.shape[:-1] + (SIDE, SIDE))
    spectra_back = conjugate(spectra)
    plane_screens = screens(wave_nums, slowness_all)
    plane_screens = plane_screens.reshape(plane_screens.shape[:-1] + (SIDE, SIDE))
    born_scale = wave_nums * STEP_DEPTH

    fields = [complex_times(plane_screens[:, 0], propagate(sources, spectra, forward, inverse))]

    def born(plane):
        scaled = born_scale[:, None, None, None] * probe_mine[None, :, plane]
        background = fields[plane]
        return jnp.stack([-scaled * background[:, None, 1], scaled * background[:, None, 0]], axis=2)

    tangent = born(0)
    for plane in range(1, plane_count):
        both = jnp.concatenate([fields[-1][:, None], tangent], axis=1)
        moved_on = complex_times(
            plane_screens[:, plane][:, None], propagate(both, spectra[:, None], forward, inverse)
        )
        fields.append(moved_on[:, 0])
        tangent = moved_on[:, 1:] + born(plane)

    adjoint = tangent
    pieces = [None] * plane_count
    for plane in reversed(range(plane_count)):
        background = fields[plane]
        product_terms = born_scale[:, None, None, None] * (
            background[:, None, 0] * adjoint[:, :, 1] - background[:, None, 1] * adjoint[:, :, 0]
        )
        pieces[plane] = jnp.sum(product_terms, axis=0)
        if plane > 0:
            turned_back = complex_times(conjugate(plane_screens[:, plane])[:, None], adjoint)
            adjoint = propagate(turned_back, spectra_back[:, None], forward, inverse)
    sketch_part = lax.optimization_barrier(jnp.stack(pieces, axis=1))
    rows, planes = sketch_part.shape[0], sketch_part.shape[1]
    by_axes = sketch_part.reshape(rows, planes, CHIPS_Y, CHIPS_Z, CORES, -1)
    slab_width = by_axes.shape[-1]
    by_axes = jnp.transpose(by_axes, (4, 3, 2, 0, 1, 5)).reshape(
        CORES, CHIPS_Z, CHIPS_Y, rows, planes * slab_width
    )
    stage_sizes = [("core", CORES), ("chip_z", CHIPS_Z), ("chip_y", CHIPS_Y)]
    row_total = planes * slab_width * src_count
    sketch_all, gram_matrix = reduce_all(
        by_axes, probe_all, stage_sizes, depth_count, group_count * src_count, row_total
    )
    depth_index = lax.axis_index("depth")
    flattened = lax.dynamic_slice_in_dim(sketch_all, depth_index * slab_width, slab_width, 1)
    local_planes = 1
    lower_factor = jnp.linalg.cholesky(gram_matrix)
    sketch_basis = lax.linalg.triangular_solve(
        lower_factor, flattened, left_side=True, lower=True
    ).reshape(probe_count, local_planes, slab_width)
    return (sketch_basis, lower_factor.T)


def solution(mesh):
    src_size, depth_size = mesh.devices.shape
    cut = mesh.devices.reshape(CHIPS_Y, CHIPS_Z, CORES, depth_size)
    fine = Mesh(cut, SRC_AXES + ("depth",))
    in_specs = (
        P(SRC_AXES, None, None, None),
        P(SRC_AXES),
        P(SRC_AXES),
        P(),
        P("depth", None),
        P(None, "depth", None),
    )
    out_specs = (P(None, "depth", SRC_AXES), P())
    return jax.shard_map(shards, mesh=fine, in_specs=in_specs, out_specs=out_specs, check_vma=False)
```

```python
import math

import jax
import jax.numpy as jnp
from jax import lax
from jax.experimental import pallas as pl
from jax.experimental.pallas import tpu as pltpu
from jax.sharding import Mesh, PartitionSpec as P

SIDE = 64
CHIPS_Y = 8
CHIPS_Z = 8
CORES = 2
SRC_AXES = ("chip_y", "chip_z", "core")


DAMPING = 0.5
STEP_DEPTH = 1.0


def dft_tables(points, direction):
    counter = jnp.arange(points, dtype=jnp.int32)
    product = counter[:, None] * counter[None, :] % points
    angles = 2.0 * math.pi / points * product.astype(jnp.float32)
    cosine = jnp.cos(angles) / math.sqrt(points)
    sine_part = direction * jnp.sin(angles) / math.sqrt(points)
    matrix = jnp.stack(
        [jnp.stack([cosine, sine_part], axis=1), jnp.stack([-sine_part, cosine], axis=1)], axis=0
    )
    matrix = matrix.astype(jnp.bfloat16)
    total_points = points * points
    twist_index = counter[:, None] * counter[None, :] % total_points
    twist_angle = 2.0 * math.pi / total_points * twist_index.astype(jnp.float32)
    return (matrix, jnp.cos(twist_angle), direction * jnp.sin(twist_angle))


def transform(values, tables):
    matrix, twist_real, twist_imag = tables
    points = matrix.shape[1]
    leading = values.shape[:-3]
    grid_values = values.reshape((-1, 2, points, points))
    segmented = jnp.einsum(
        "nrab,rasc->nscb", grid_values, matrix, preferred_element_type=jnp.float32
    )
    real_part = segmented[:, 0]
    imag_part = segmented[:, 1]
    turned = jnp.stack(
        [
            real_part * twist_real - imag_part * twist_imag,
            real_part * twist_imag + imag_part * twist_real,
        ],
        axis=1,
    ).astype(jnp.bfloat16)
    result = jnp.einsum("nscb,sbtd->ntdc", turned, matrix, preferred_element_type=jnp.float32)
    return result.reshape(leading + (2, points, points))


def complex_times(first, second):
    real_part = first[..., 0, :, :] * second[..., 0, :, :] - first[..., 1, :, :] * second[..., 1, :, :]
    imag_part = first[..., 0, :, :] * second[..., 1, :, :] + first[..., 1, :, :] * second[..., 0, :, :]
    return jnp.stack([real_part, imag_part], axis=-3)


def conjugate(values):
    return jnp.stack([values[..., 0, :, :], -values[..., 1, :, :]], axis=-3)


def propagate(values, spectrum, forward, inverse):
    moved_on = transform(values.astype(jnp.bfloat16), forward)
    return transform(complex_times(moved_on, spectrum).astype(jnp.bfloat16), inverse)


def propagator(wave_nums, points_all):
    counter = jnp.arange(points_all, dtype=jnp.int32)
    folded = jnp.where(counter < points_all // 2, counter, counter - points_all).astype(jnp.float32)
    lateral = 2.0 * math.pi / points_all * folded
    excess = wave_nums[:, None] ** 2 - lateral[None, :] ** 2
    upward = jnp.sqrt(jnp.maximum(excess, 0.0)) * STEP_DEPTH
    damped = jnp.sqrt(jnp.maximum(-excess, 0.0)) * STEP_DEPTH
    real_part = jnp.where(excess > 0, jnp.cos(upward), jnp.exp(-damped))
    imag_part = jnp.where(excess > 0, jnp.sin(upward), jnp.zeros_like(upward))
    return jnp.stack([real_part, imag_part], axis=1)


def screens(wave_nums, slowness):
    phase = wave_nums[:, None, None] * STEP_DEPTH * slowness[None]
    return jnp.stack([jnp.cos(phase), jnp.sin(phase)], axis=2)


def encoded_sources(incident, encode, sources):
    shifts = jnp.arange(sources, dtype=jnp.int32)
    bit_set = encode[:, None] >> shifts[None, :] & 1
    signs_all = (1 - 2 * bit_set).astype(jnp.float32)
    return jnp.sum(signs_all[:, :, None, None] * incident, axis=1)


def lookup_waves(freq_index, wavenum, table_size):
    onehot_rows = (freq_index[:, None] == jnp.arange(table_size, dtype=jnp.int32)[None, :]).astype(
        jnp.float32
    )
    return jnp.sum(onehot_rows * wavenum[None, :], axis=1)


def exchange(axis, size, current, slot, send_sems, recv_sems, offset, whole=False, pieces=1):
    me = lax.axis_index(axis)

    def copy_of(peer, piece, slot_index, source):
        block = current if whole else current.at[source]
        target = slot.at[slot_index]
        if pieces > 1:
            block, target = block.at[piece], target.at[piece]
        return pltpu.make_async_remote_copy(
            src_ref=block,
            dst_ref=target,
            send_sem=send_sems.at[offset + source * pieces + piece],
            recv_sem=recv_sems.at[offset + slot_index * pieces + piece],
            device_id={axis: peer},
            device_id_type=pl.DeviceIdType.MESH,
        )

    copies = []
    for step in range(1, size):
        peer = lax.rem(me + step, size)
        for piece in range(pieces):
            copy = copy_of(peer, piece, me, peer)
            copy.start()
            copies.append(copy)
    for copy in copies:
        copy.wait_send()
    for step in range(1, size):
        sender = lax.rem(me + size - step, size)
        for piece in range(pieces):
            copy_of(sender, piece, sender, sender).wait_recv()
    return me


def reduce_kernel(stages, depth_size, divisor, row_total, part_ref, probe_ref, sketch_ref, gram_ref,
                  *scratch):
    count = len(stages)
    slots = scratch[:count]
    sums = scratch[count : 2 * count - 1]
    gram_slots = scratch[2 * count - 1 : 3 * count - 1]
    mine, gathered, carried, send_sems, recv_sems = scratch[3 * count - 1 :]
    barrier = pltpu.get_barrier_semaphore()
    peers_total = 0
    for axis, size in stages + [("depth", depth_size)]:
        me = lax.axis_index(axis)
        for step in range(1, size):
            pl.semaphore_signal(barrier, inc=1, device_id={axis: lax.rem(me + step, size)},
                                device_id_type=pl.DeviceIdType.MESH)
            peers_total += 1
    pl.semaphore_wait(barrier, peers_total)
    current = part_ref
    offset = 0
    for stage, (axis, size) in enumerate(stages):
        pieces = current.shape[1] if stage == 0 else 1
        me = exchange(axis, size, current, slots[stage], send_sems, recv_sems, offset, pieces=pieces)
        offset += size * pieces
        total = current[me]
        for step in range(1, size):
            total = total + slots[stage][lax.rem(me + size - step, size)]
        if stage + 1 < count:
            sums[stage][...] = total
            current = sums[stage]
        else:
            mine[...] = total
    me = exchange("depth", depth_size, mine, gathered, send_sems, recv_sems, offset, whole=True)
    offset += depth_size
    gathered[me] = mine[...]
    summed = gathered[...].reshape(sketch_ref.shape)
    sketch = summed / divisor + DAMPING * probe_ref[...]
    sketch_ref[...] = sketch
    carried[...] = lax.dot_general(
        sketch, sketch, (((1,), (1,)), ((), ())), precision=lax.Precision.HIGHEST,
        preferred_element_type=jnp.float32,
    ) / row_total
    for stage, (axis, size) in enumerate(stages):
        slot = gram_slots[stage]
        me = exchange(axis, size, carried, slot, send_sems, recv_sems, offset, whole=True)
        offset += size
        slot[me] = carried[...]
        total = slot[0]
        for member in range(1, size):
            total = total + slot[member]
        carried[...] = total
    gram_ref[...] = carried[...]


def reduce_all(part, probe_all, stages, depth_size, divisor, row_total):
    stages = [(axis, size) for axis, size in stages if size > 1]
    part = part.reshape(tuple(size for _, size in stages) + part.shape[-2:])
    rows, width = probe_all.shape
    scratch = [pltpu.VMEM(part.shape[stage:], jnp.float32) for stage in range(len(stages))]
    scratch += [pltpu.VMEM(part.shape[stage + 1 :], jnp.float32) for stage in range(len(stages) - 1)]
    scratch += [pltpu.VMEM((size, rows, rows), jnp.float32) for _, size in stages]
    semaphores = 2 * sum(size for _, size in stages) + depth_size + stages[0][1] * part.shape[1]
    scratch += [
        pltpu.VMEM(part.shape[-2:], jnp.float32),
        pltpu.VMEM((depth_size,) + part.shape[-2:], jnp.float32),
        pltpu.VMEM((rows, rows), jnp.float32),
        pltpu.SemaphoreType.DMA((semaphores,)),
        pltpu.SemaphoreType.DMA((semaphores,)),
    ]
    return pl.pallas_call(
        lambda *refs: reduce_kernel(stages, depth_size, divisor, row_total, *refs),
        out_shape=(
            jax.ShapeDtypeStruct((rows, width), jnp.float32),
            jax.ShapeDtypeStruct((rows, rows), jnp.float32),
        ),
        in_specs=[pl.BlockSpec(memory_space=pltpu.VMEM)] * 2,
        out_specs=(pl.BlockSpec(memory_space=pltpu.VMEM), pl.BlockSpec(memory_space=pltpu.VMEM)),
        scratch_shapes=scratch,
        compiler_params=pltpu.CompilerParams(collective_id=2, has_side_effects=True),
    )(part, probe_all)


def shards(incident, encode, freq_index, wavenum, slowness, probes):
    points_all = SIDE * SIDE
    forward = dft_tables(SIDE, -1.0)
    inverse = dft_tables(SIDE, 1.0)
    group_count = incident.shape[0]
    probe_count = probes.shape[0]
    src_count = lax.axis_size(SRC_AXES)
    depth_count = lax.axis_size("depth")
    rows = probe_count // depth_count
    points = probes.shape[2]
    slab_points = points // src_count
    probe_slab = lax.dynamic_slice_in_dim(
        probes, lax.axis_index(SRC_AXES) * slab_points, slab_points, 2
    )
    high = slowness.astype(jnp.bfloat16)
    rest = slowness - high.astype(jnp.float32)
    middle = rest.astype(jnp.bfloat16)
    low = (rest - middle.astype(jnp.float32)).astype(jnp.bfloat16)
    shared = jnp.concatenate([probe_slab.reshape(-1), high.reshape(-1), middle.reshape(-1), low.reshape(-1)])
    payload = jnp.concatenate(
        [probes.reshape(depth_count, -1), jnp.broadcast_to(shared[None], (depth_count,) + shared.shape)],
        axis=1,
    )
    payload = lax.all_to_all(payload, "depth", 0, 0, tiled=True)
    cut = rows * points
    probe_mine = jnp.transpose(payload[:, :cut].reshape(depth_count, rows, points), (1, 0, 2))
    probe_mine = probe_mine.astype(jnp.float32)
    probe_mine = probe_mine.reshape(probe_mine.shape[:2] + (SIDE, SIDE))
    slab_size = probe_count * slab_points
    probe_all = payload[:, cut : cut + slab_size].reshape(depth_count, probe_count, slab_points)
    probe_all = jnp.transpose(probe_all, (1, 0, 2)).reshape(probe_count, -1).astype(jnp.float32)
    parts = payload[:, cut + slab_size :].reshape(depth_count, 3, points).astype(jnp.float32)
    slowness_all = (parts[:, 0] + parts[:, 1]) + parts[:, 2]
    plane_count = slowness_all.shape[0]
    sources = encoded_sources(incident, encode, incident.shape[1])
    sources = sources.reshape(sources.shape[:-1] + (SIDE, SIDE))
    wave_nums = lookup_waves(freq_index, wavenum, wavenum.shape[0])
    spectra = propagator(wave_nums, points_all)
    spectra = spectra.reshape(spectra.shape[:-1] + (SIDE, SIDE))
    spectra_back = conjugate(spectra)
    plane_screens = screens(wave_nums, slowness_all)
    plane_screens = plane_screens.reshape(plane_screens.shape[:-1] + (SIDE, SIDE))
    born_scale = wave_nums * STEP_DEPTH

    fields = [complex_times(plane_screens[:, 0], propagate(sources, spectra, forward, inverse))]

    def born(plane):
        scaled = born_scale[:, None, None, None] * probe_mine[None, :, plane]
        background = fields[plane]
        return jnp.stack([-scaled * background[:, None, 1], scaled * background[:, None, 0]], axis=2)

    tangent = born(0)
    for plane in range(1, plane_count):
        both = jnp.concatenate([fields[-1][:, None], tangent], axis=1)
        moved_on = complex_times(
            plane_screens[:, plane][:, None], propagate(both, spectra[:, None], forward, inverse)
        )
        fields.append(moved_on[:, 0])
        tangent = moved_on[:, 1:] + born(plane)

    adjoint = tangent
    pieces = [None] * plane_count
    for plane in reversed(range(plane_count)):
        background = fields[plane]
        product_terms = born_scale[:, None, None, None] * (
            background[:, None, 0] * adjoint[:, :, 1] - background[:, None, 1] * adjoint[:, :, 0]
        )
        pieces[plane] = jnp.sum(product_terms, axis=0)
        if plane > 0:
            turned_back = complex_times(conjugate(plane_screens[:, plane])[:, None], adjoint)
            adjoint = propagate(turned_back, spectra_back[:, None], forward, inverse)
    sketch_part = lax.optimization_barrier(jnp.stack(pieces, axis=1))
    rows, planes = sketch_part.shape[0], sketch_part.shape[1]
    by_axes = sketch_part.reshape(rows, planes, CHIPS_Y, CHIPS_Z, CORES, -1)
    slab_width = by_axes.shape[-1]
    by_axes = jnp.transpose(by_axes, (4, 3, 2, 0, 1, 5)).reshape(
        CORES, CHIPS_Z, CHIPS_Y, rows, planes * slab_width
    )
    stage_sizes = [("core", CORES), ("chip_z", CHIPS_Z), ("chip_y", CHIPS_Y)]
    row_total = planes * slab_width * src_count
    sketch_all, gram_matrix = reduce_all(
        by_axes, probe_all, stage_sizes, depth_count, group_count * src_count, row_total
    )
    depth_index = lax.axis_index("depth")
    flattened = lax.dynamic_slice_in_dim(sketch_all, depth_index * slab_width, slab_width, 1)
    local_planes = 1
    lower_factor = jnp.linalg.cholesky(gram_matrix)
    sketch_basis = lax.linalg.triangular_solve(
        lower_factor, flattened, left_side=True, lower=True
    ).reshape(probe_count, local_planes, slab_width)
    return (sketch_basis, lower_factor.T)


def solution(mesh):
    src_size, depth_size = mesh.devices.shape
    cut = mesh.devices.reshape(CHIPS_Y, CHIPS_Z, CORES, depth_size)
    fine = Mesh(cut, SRC_AXES + ("depth",))
    in_specs = (
        P(SRC_AXES, None, None, None),
        P(SRC_AXES),
        P(SRC_AXES),
        P(),
        P("depth", None),
        P(None, "depth", None),
    )
    out_specs = (P(None, "depth", SRC_AXES), P())
    return jax.shard_map(shards, mesh=fine, in_specs=in_specs, out_specs=out_specs, check_vma=False)
```

```python
import math

import jax
import jax.numpy as jnp
from jax import lax
from jax.experimental import pallas as pl
from jax.experimental.pallas import tpu as pltpu
from jax.sharding import Mesh, PartitionSpec as P

SIDE = 64
CHIPS_Y = 8
CHIPS_Z = 8
CORES = 2
SRC_AXES = ("chip_y", "chip_z", "core")


DAMPING = 0.5
STEP_DEPTH = 1.0


def dft_tables(points, direction):
    counter = jnp.arange(points, dtype=jnp.int32)
    product = counter[:, None] * counter[None, :] % points
    angles = 2.0 * math.pi / points * product.astype(jnp.float32)
    cosine = jnp.cos(angles) / math.sqrt(points)
    sine_part = direction * jnp.sin(angles) / math.sqrt(points)
    matrix = jnp.stack(
        [jnp.stack([cosine, sine_part], axis=1), jnp.stack([-sine_part, cosine], axis=1)], axis=0
    )
    matrix = matrix.astype(jnp.bfloat16)
    total_points = points * points
    twist_index = counter[:, None] * counter[None, :] % total_points
    twist_angle = 2.0 * math.pi / total_points * twist_index.astype(jnp.float32)
    return (matrix, jnp.cos(twist_angle), direction * jnp.sin(twist_angle))


def transform(values, tables):
    matrix, twist_real, twist_imag = tables
    points = matrix.shape[1]
    leading = values.shape[:-3]
    grid_values = values.reshape((-1, 2, points, points))
    segmented = jnp.einsum(
        "nrab,rasc->nscb", grid_values, matrix, preferred_element_type=jnp.float32
    )
    real_part = segmented[:, 0]
    imag_part = segmented[:, 1]
    turned = jnp.stack(
        [
            real_part * twist_real - imag_part * twist_imag,
            real_part * twist_imag + imag_part * twist_real,
        ],
        axis=1,
    ).astype(jnp.bfloat16)
    result = jnp.einsum("nscb,sbtd->ntdc", turned, matrix, preferred_element_type=jnp.float32)
    return result.reshape(leading + (2, points, points))


def complex_times(first, second):
    real_part = first[..., 0, :, :] * second[..., 0, :, :] - first[..., 1, :, :] * second[..., 1, :, :]
    imag_part = first[..., 0, :, :] * second[..., 1, :, :] + first[..., 1, :, :] * second[..., 0, :, :]
    return jnp.stack([real_part, imag_part], axis=-3)


def conjugate(values):
    return jnp.stack([values[..., 0, :, :], -values[..., 1, :, :]], axis=-3)


def propagate(values, spectrum, forward, inverse):
    moved_on = transform(values.astype(jnp.bfloat16), forward)
    return transform(complex_times(moved_on, spectrum).astype(jnp.bfloat16), inverse)


def propagator(wave_nums, points_all):
    counter = jnp.arange(points_all, dtype=jnp.int32)
    folded = jnp.where(counter < points_all // 2, counter, counter - points_all).astype(jnp.float32)
    lateral = 2.0 * math.pi / points_all * folded
    excess = wave_nums[:, None] ** 2 - lateral[None, :] ** 2
    upward = jnp.sqrt(jnp.maximum(excess, 0.0)) * STEP_DEPTH
    damped = jnp.sqrt(jnp.maximum(-excess, 0.0)) * STEP_DEPTH
    real_part = jnp.where(excess > 0, jnp.cos(upward), jnp.exp(-damped))
    imag_part = jnp.where(excess > 0, jnp.sin(upward), jnp.zeros_like(upward))
    return jnp.stack([real_part, imag_part], axis=1)


def screens(wave_nums, slowness):
    phase = wave_nums[:, None, None] * STEP_DEPTH * slowness[None]
    return jnp.stack([jnp.cos(phase), jnp.sin(phase)], axis=2)


def encoded_sources(incident, encode, sources):
    shifts = jnp.arange(sources, dtype=jnp.int32)
    bit_set = encode[:, None] >> shifts[None, :] & 1
    signs_all = (1 - 2 * bit_set).astype(jnp.float32)
    return jnp.sum(signs_all[:, :, None, None] * incident, axis=1)


def lookup_waves(freq_index, wavenum, table_size):
    onehot_rows = (freq_index[:, None] == jnp.arange(table_size, dtype=jnp.int32)[None, :]).astype(
        jnp.float32
    )
    return jnp.sum(onehot_rows * wavenum[None, :], axis=1)


def exchange(axis, size, current, slot, send_sems, recv_sems, offset, whole=False):
    me = lax.axis_index(axis)
    copies = []
    for step in range(1, size):
        peer = lax.rem(me + step, size)
        copy = pltpu.make_async_remote_copy(
            src_ref=current if whole else current.at[peer],
            dst_ref=slot.at[me],
            send_sem=send_sems.at[offset + peer],
            recv_sem=recv_sems.at[offset + me],
            device_id={axis: peer},
            device_id_type=pl.DeviceIdType.MESH,
        )
        copy.start()
        copies.append(copy)
    for copy in copies:
        copy.wait_send()
    for step in range(1, size):
        sender = lax.rem(me + size - step, size)
        incoming = pltpu.make_async_remote_copy(
            src_ref=current if whole else current.at[sender],
            dst_ref=slot.at[sender],
            send_sem=send_sems.at[offset + sender],
            recv_sem=recv_sems.at[offset + sender],
            device_id={axis: sender},
            device_id_type=pl.DeviceIdType.MESH,
        )
        incoming.wait_recv()
    return me


def reduce_kernel(stages, depth_size, divisor, row_total, part_ref, probe_ref, sketch_ref, gram_ref,
                  *scratch):
    count = len(stages)
    slots = scratch[:count]
    sums = scratch[count : 2 * count - 1]
    gram_slots = scratch[2 * count - 1 : 3 * count - 1]
    mine, gathered, carried, send_sems, recv_sems = scratch[3 * count - 1 :]
    barrier = pltpu.get_barrier_semaphore()
    peers_total = 0
    for axis, size in stages + [("depth", depth_size)]:
        me = lax.axis_index(axis)
        for step in range(1, size):
            pl.semaphore_signal(barrier, inc=1, device_id={axis: lax.rem(me + step, size)},
                                device_id_type=pl.DeviceIdType.MESH)
            peers_total += 1
    pl.semaphore_wait(barrier, peers_total)
    current = part_ref
    offset = 0
    for stage, (axis, size) in enumerate(stages):
        me = exchange(axis, size, current, slots[stage], send_sems, recv_sems, offset)
        offset += size
        total = current[me]
        for step in range(1, size):
            total = total + slots[stage][lax.rem(me + size - step, size)]
        if stage + 1 < count:
            sums[stage][...] = total
            current = sums[stage]
        else:
            mine[...] = total
    me = exchange("depth", depth_size, mine, gathered, send_sems, recv_sems, offset, whole=True)
    offset += depth_size
    gathered[me] = mine[...]
    summed = gathered[...].reshape(sketch_ref.shape)
    sketch = summed / divisor + DAMPING * probe_ref[...]
    sketch_ref[...] = sketch
    carried[...] = lax.dot_general(
        sketch, sketch, (((1,), (1,)), ((), ())), precision=lax.Precision.HIGHEST,
        preferred_element_type=jnp.float32,
    ) / row_total
    for stage, (axis, size) in enumerate(stages):
        slot = gram_slots[stage]
        me = exchange(axis, size, carried, slot, send_sems, recv_sems, offset, whole=True)
        offset += size
        slot[me] = carried[...]
        total = slot[0]
        for member in range(1, size):
            total = total + slot[member]
        carried[...] = total
    gram_ref[...] = carried[...]


def reduce_all(part, probe_all, stages, depth_size, divisor, row_total):
    stages = [(axis, size) for axis, size in stages if size > 1]
    part = part.reshape(tuple(size for _, size in stages) + part.shape[-2:])
    rows, width = probe_all.shape
    scratch = [pltpu.VMEM(part.shape[stage:], jnp.float32) for stage in range(len(stages))]
    scratch += [pltpu.VMEM(part.shape[stage + 1 :], jnp.float32) for stage in range(len(stages) - 1)]
    scratch += [pltpu.VMEM((size, rows, rows), jnp.float32) for _, size in stages]
    semaphores = 2 * sum(size for _, size in stages) + depth_size
    scratch += [
        pltpu.VMEM(part.shape[-2:], jnp.float32),
        pltpu.VMEM((depth_size,) + part.shape[-2:], jnp.float32),
        pltpu.VMEM((rows, rows), jnp.float32),
        pltpu.SemaphoreType.DMA((semaphores,)),
        pltpu.SemaphoreType.DMA((semaphores,)),
    ]
    return pl.pallas_call(
        lambda *refs: reduce_kernel(stages, depth_size, divisor, row_total, *refs),
        out_shape=(
            jax.ShapeDtypeStruct((rows, width), jnp.float32),
            jax.ShapeDtypeStruct((rows, rows), jnp.float32),
        ),
        in_specs=[pl.BlockSpec(memory_space=pltpu.VMEM)] * 2,
        out_specs=(pl.BlockSpec(memory_space=pltpu.VMEM), pl.BlockSpec(memory_space=pltpu.VMEM)),
        scratch_shapes=scratch,
        compiler_params=pltpu.CompilerParams(collective_id=2, has_side_effects=True),
    )(part, probe_all)


def shards(incident, encode, freq_index, wavenum, slowness, probes):
    points_all = SIDE * SIDE
    forward = dft_tables(SIDE, -1.0)
    inverse = dft_tables(SIDE, 1.0)
    group_count = incident.shape[0]
    probe_count = probes.shape[0]
    src_count = lax.axis_size(SRC_AXES)
    depth_count = lax.axis_size("depth")
    rows = probe_count // depth_count
    points = probes.shape[2]
    slab_points = points // src_count
    probe_slab = lax.dynamic_slice_in_dim(
        probes, lax.axis_index(SRC_AXES) * slab_points, slab_points, 2
    )
    high = slowness.astype(jnp.bfloat16)
    rest = slowness - high.astype(jnp.float32)
    middle = rest.astype(jnp.bfloat16)
    low = (rest - middle.astype(jnp.float32)).astype(jnp.bfloat16)
    shared = jnp.concatenate([probe_slab.reshape(-1), high.reshape(-1), middle.reshape(-1), low.reshape(-1)])
    payload = jnp.concatenate(
        [probes.reshape(depth_count, -1), jnp.broadcast_to(shared[None], (depth_count,) + shared.shape)],
        axis=1,
    )
    payload = lax.all_to_all(payload, "depth", 0, 0, tiled=True)
    cut = rows * points
    probe_mine = jnp.transpose(payload[:, :cut].reshape(depth_count, rows, points), (1, 0, 2))
    probe_mine = probe_mine.astype(jnp.float32)
    probe_mine = probe_mine.reshape(probe_mine.shape[:2] + (SIDE, SIDE))
    slab_size = probe_count * slab_points
    probe_all = payload[:, cut : cut + slab_size].reshape(depth_count, probe_count, slab_points)
    probe_all = jnp.transpose(probe_all, (1, 0, 2)).reshape(probe_count, -1).astype(jnp.float32)
    parts = payload[:, cut + slab_size :].reshape(depth_count, 3, points).astype(jnp.float32)
    slowness_all = (parts[:, 0] + parts[:, 1]) + parts[:, 2]
    plane_count = slowness_all.shape[0]
    sources = encoded_sources(incident, encode, incident.shape[1])
    sources = sources.reshape(sources.shape[:-1] + (SIDE, SIDE))
    wave_nums = lookup_waves(freq_index, wavenum, wavenum.shape[0])
    spectra = propagator(wave_nums, points_all)
    spectra = spectra.reshape(spectra.shape[:-1] + (SIDE, SIDE))
    spectra_back = conjugate(spectra)
    plane_screens = screens(wave_nums, slowness_all)
    plane_screens = plane_screens.reshape(plane_screens.shape[:-1] + (SIDE, SIDE))
    born_scale = wave_nums * STEP_DEPTH

    fields = [complex_times(plane_screens[:, 0], propagate(sources, spectra, forward, inverse))]

    def born(plane):
        scaled = born_scale[:, None, None, None] * probe_mine[None, :, plane]
        background = fields[plane]
        return jnp.stack([-scaled * background[:, None, 1], scaled * background[:, None, 0]], axis=2)

    tangent = born(0)
    for plane in range(1, plane_count):
        both = jnp.concatenate([fields[-1][:, None], tangent], axis=1)
        moved_on = complex_times(
            plane_screens[:, plane][:, None], propagate(both, spectra[:, None], forward, inverse)
        )
        fields.append(moved_on[:, 0])
        tangent = moved_on[:, 1:] + born(plane)

    adjoint = tangent
    pieces = [None] * plane_count
    for plane in reversed(range(plane_count)):
        background = fields[plane]
        product_terms = born_scale[:, None, None, None] * (
            background[:, None, 0] * adjoint[:, :, 1] - background[:, None, 1] * adjoint[:, :, 0]
        )
        pieces[plane] = jnp.sum(product_terms, axis=0)
        if plane > 0:
            turned_back = complex_times(conjugate(plane_screens[:, plane])[:, None], adjoint)
            adjoint = propagate(turned_back, spectra_back[:, None], forward, inverse)
    sketch_part = lax.optimization_barrier(jnp.stack(pieces, axis=1))
    rows, planes = sketch_part.shape[0], sketch_part.shape[1]
    by_axes = sketch_part.reshape(rows, planes, CHIPS_Y, CHIPS_Z, CORES, -1)
    slab_width = by_axes.shape[-1]
    by_axes = jnp.transpose(by_axes, (4, 3, 2, 0, 1, 5)).reshape(
        CORES, CHIPS_Z, CHIPS_Y, rows, planes * slab_width
    )
    stage_sizes = [("core", CORES), ("chip_z", CHIPS_Z), ("chip_y", CHIPS_Y)]
    row_total = planes * slab_width * src_count
    sketch_all, gram_matrix = reduce_all(
        by_axes, probe_all, stage_sizes, depth_count, group_count * src_count, row_total
    )
    depth_index = lax.axis_index("depth")
    flattened = lax.dynamic_slice_in_dim(sketch_all, depth_index * slab_width, slab_width, 1)
    local_planes = 1
    lower_factor = lax.linalg.cholesky(gram_matrix, symmetrize_input=False)
    sketch_basis = lax.linalg.triangular_solve(
        lower_factor, flattened, left_side=True, lower=True
    ).reshape(probe_count, local_planes, slab_width)
    return (sketch_basis, lower_factor.T)


def solution(mesh):
    src_size, depth_size = mesh.devices.shape
    cut = mesh.devices.reshape(CHIPS_Y, CHIPS_Z, CORES, depth_size)
    fine = Mesh(cut, SRC_AXES + ("depth",))
    in_specs = (
        P(SRC_AXES, None, None, None),
        P(SRC_AXES),
        P(SRC_AXES),
        P(),
        P("depth", None),
        P(None, "depth", None),
    )
    out_specs = (P(None, "depth", SRC_AXES), P())
    return jax.shard_map(shards, mesh=fine, in_specs=in_specs, out_specs=out_specs, check_vma=False)
```

```python
import math

import jax
import jax.numpy as jnp
from jax import lax
from jax.experimental import pallas as pl
from jax.experimental.pallas import tpu as pltpu
from jax.sharding import Mesh, PartitionSpec as P

SIDE = 64
CHIPS_Y = 8
CHIPS_Z = 8
CORES = 2
SRC_AXES = ("chip_y", "chip_z", "core")


DAMPING = 0.5
STEP_DEPTH = 1.0


def dft_tables(points, direction):
    counter = jnp.arange(points, dtype=jnp.int32)
    product = counter[:, None] * counter[None, :] % points
    angles = 2.0 * math.pi / points * product.astype(jnp.float32)
    cosine = jnp.cos(angles) / math.sqrt(points)
    sine_part = direction * jnp.sin(angles) / math.sqrt(points)
    matrix = jnp.stack(
        [jnp.stack([cosine, sine_part], axis=1), jnp.stack([-sine_part, cosine], axis=1)], axis=0
    )
    matrix = matrix.astype(jnp.bfloat16)
    total_points = points * points
    twist_index = counter[:, None] * counter[None, :] % total_points
    twist_angle = 2.0 * math.pi / total_points * twist_index.astype(jnp.float32)
    return (matrix, jnp.cos(twist_angle), direction * jnp.sin(twist_angle))


def transform(values, tables):
    matrix, twist_real, twist_imag = tables
    points = matrix.shape[1]
    leading = values.shape[:-3]
    grid_values = values.reshape((-1, 2, points, points))
    segmented = jnp.einsum(
        "nrab,rasc->nscb", grid_values, matrix, preferred_element_type=jnp.float32
    )
    real_part = segmented[:, 0]
    imag_part = segmented[:, 1]
    turned = jnp.stack(
        [
            real_part * twist_real - imag_part * twist_imag,
            real_part * twist_imag + imag_part * twist_real,
        ],
        axis=1,
    ).astype(jnp.bfloat16)
    result = jnp.einsum("nscb,sbtd->ntdc", turned, matrix, preferred_element_type=jnp.float32)
    return result.reshape(leading + (2, points, points))


def complex_times(first, second):
    real_part = first[..., 0, :, :] * second[..., 0, :, :] - first[..., 1, :, :] * second[..., 1, :, :]
    imag_part = first[..., 0, :, :] * second[..., 1, :, :] + first[..., 1, :, :] * second[..., 0, :, :]
    return jnp.stack([real_part, imag_part], axis=-3)


def conjugate(values):
    return jnp.stack([values[..., 0, :, :], -values[..., 1, :, :]], axis=-3)


def propagate(values, spectrum, forward, inverse):
    moved_on = transform(values.astype(jnp.bfloat16), forward)
    return transform(complex_times(moved_on, spectrum).astype(jnp.bfloat16), inverse)


def propagator(wave_nums, points_all):
    counter = jnp.arange(points_all, dtype=jnp.int32)
    folded = jnp.where(counter < points_all // 2, counter, counter - points_all).astype(jnp.float32)
    lateral = 2.0 * math.pi / points_all * folded
    excess = wave_nums[:, None] ** 2 - lateral[None, :] ** 2
    upward = jnp.sqrt(jnp.maximum(excess, 0.0)) * STEP_DEPTH
    damped = jnp.sqrt(jnp.maximum(-excess, 0.0)) * STEP_DEPTH
    real_part = jnp.where(excess > 0, jnp.cos(upward), jnp.exp(-damped))
    imag_part = jnp.where(excess > 0, jnp.sin(upward), jnp.zeros_like(upward))
    return jnp.stack([real_part, imag_part], axis=1)


def screens(wave_nums, slowness):
    phase = wave_nums[:, None, None] * STEP_DEPTH * slowness[None]
    return jnp.stack([jnp.cos(phase), jnp.sin(phase)], axis=2)


def encoded_sources(incident, encode, sources):
    shifts = jnp.arange(sources, dtype=jnp.int32)
    bit_set = encode[:, None] >> shifts[None, :] & 1
    signs_all = (1 - 2 * bit_set).astype(jnp.float32)
    return jnp.sum(signs_all[:, :, None, None] * incident, axis=1)


def lookup_waves(freq_index, wavenum, table_size):
    onehot_rows = (freq_index[:, None] == jnp.arange(table_size, dtype=jnp.int32)[None, :]).astype(
        jnp.float32
    )
    return jnp.sum(onehot_rows * wavenum[None, :], axis=1)


def exchange(axis, size, current, slot, send_sems, recv_sems, offset, whole=False):
    me = lax.axis_index(axis)
    copies = []
    for step in range(1, size):
        peer = lax.rem(me + step, size)
        copy = pltpu.make_async_remote_copy(
            src_ref=current if whole else current.at[peer],
            dst_ref=slot.at[me],
            send_sem=send_sems.at[offset + peer],
            recv_sem=recv_sems.at[offset + me],
            device_id={axis: peer},
            device_id_type=pl.DeviceIdType.MESH,
        )
        copy.start()
        copies.append(copy)
    for copy in copies:
        copy.wait_send()
    for step in range(1, size):
        sender = lax.rem(me + size - step, size)
        incoming = pltpu.make_async_remote_copy(
            src_ref=current if whole else current.at[sender],
            dst_ref=slot.at[sender],
            send_sem=send_sems.at[offset + sender],
            recv_sem=recv_sems.at[offset + sender],
            device_id={axis: sender},
            device_id_type=pl.DeviceIdType.MESH,
        )
        incoming.wait_recv()
    return me


def reduce_kernel(stages, depth_size, divisor, row_total, part_ref, probe_ref, sketch_ref, gram_ref,
                  *scratch):
    count = len(stages)
    slots = scratch[:count]
    sums = scratch[count : 2 * count - 1]
    gram_slots = scratch[2 * count - 1 : 3 * count - 1]
    mine, gathered, carried, send_sems, recv_sems = scratch[3 * count - 1 :]
    barrier = pltpu.get_barrier_semaphore()
    peers_total = 0
    for axis, size in stages + [("depth", depth_size)]:
        me = lax.axis_index(axis)
        for step in range(1, size):
            pl.semaphore_signal(barrier, inc=1, device_id={axis: lax.rem(me + step, size)},
                                device_id_type=pl.DeviceIdType.MESH)
            peers_total += 1
    pl.semaphore_wait(barrier, peers_total)
    current = part_ref
    offset = 0
    for stage, (axis, size) in enumerate(stages):
        me = exchange(axis, size, current, slots[stage], send_sems, recv_sems, offset)
        offset += size
        total = current[me]
        for step in range(1, size):
            total = total + slots[stage][lax.rem(me + size - step, size)]
        if stage + 1 < count:
            sums[stage][...] = total
            current = sums[stage]
        else:
            mine[...] = total
    me = exchange("depth", depth_size, mine, gathered, send_sems, recv_sems, offset, whole=True)
    offset += depth_size
    gathered[me] = mine[...]
    summed = gathered[...].reshape(sketch_ref.shape)
    sketch = summed / divisor + DAMPING * probe_ref[...]
    sketch_ref[...] = sketch
    carried[...] = lax.dot_general(
        sketch, sketch, (((1,), (1,)), ((), ())), precision=lax.Precision.HIGHEST,
        preferred_element_type=jnp.float32,
    ) / row_total
    for stage, (axis, size) in enumerate(stages):
        slot = gram_slots[stage]
        me = exchange(axis, size, carried, slot, send_sems, recv_sems, offset, whole=True)
        offset += size
        slot[me] = carried[...]
        total = slot[0]
        for member in range(1, size):
            total = total + slot[member]
        carried[...] = total
    gram_ref[...] = carried[...]


def reduce_all(part, probe_all, stages, depth_size, divisor, row_total):
    stages = [(axis, size) for axis, size in stages if size > 1]
    part = part.reshape(tuple(size for _, size in stages) + part.shape[-2:])
    rows, width = probe_all.shape
    scratch = [pltpu.VMEM(part.shape[stage:], jnp.float32) for stage in range(len(stages))]
    scratch += [pltpu.VMEM(part.shape[stage + 1 :], jnp.float32) for stage in range(len(stages) - 1)]
    scratch += [pltpu.VMEM((size, rows, rows), jnp.float32) for _, size in stages]
    semaphores = 2 * sum(size for _, size in stages) + depth_size
    scratch += [
        pltpu.VMEM(part.shape[-2:], jnp.float32),
        pltpu.VMEM((depth_size,) + part.shape[-2:], jnp.float32),
        pltpu.VMEM((rows, rows), jnp.float32),
        pltpu.SemaphoreType.DMA((semaphores,)),
        pltpu.SemaphoreType.DMA((semaphores,)),
    ]
    return pl.pallas_call(
        lambda *refs: reduce_kernel(stages, depth_size, divisor, row_total, *refs),
        out_shape=(
            jax.ShapeDtypeStruct((rows, width), jnp.float32),
            jax.ShapeDtypeStruct((rows, rows), jnp.float32),
        ),
        in_specs=[pl.BlockSpec(memory_space=pltpu.VMEM)] * 2,
        out_specs=(pl.BlockSpec(memory_space=pltpu.VMEM), pl.BlockSpec(memory_space=pltpu.VMEM)),
        scratch_shapes=scratch,
        compiler_params=pltpu.CompilerParams(collective_id=2, has_side_effects=True),
    )(part, probe_all)


def shards(incident, encode, freq_index, wavenum, slowness, probes):
    points_all = SIDE * SIDE
    forward = dft_tables(SIDE, -1.0)
    inverse = dft_tables(SIDE, 1.0)
    group_count = incident.shape[0]
    probe_count = probes.shape[0]
    src_count = lax.axis_size(SRC_AXES)
    depth_count = lax.axis_size("depth")
    rows = probe_count // depth_count
    points = probes.shape[2]
    slab_points = points // src_count
    probe_slab = lax.dynamic_slice_in_dim(
        probes, lax.axis_index(SRC_AXES) * slab_points, slab_points, 2
    )
    high = slowness.astype(jnp.bfloat16)
    rest = slowness - high.astype(jnp.float32)
    middle = rest.astype(jnp.bfloat16)
    low = (rest - middle.astype(jnp.float32)).astype(jnp.bfloat16)
    shared = jnp.concatenate([probe_slab.reshape(-1), high.reshape(-1), middle.reshape(-1), low.reshape(-1)])
    payload = jnp.concatenate(
        [probes.reshape(depth_count, -1), jnp.broadcast_to(shared[None], (depth_count,) + shared.shape)],
        axis=1,
    )
    payload = lax.all_to_all(payload, "depth", 0, 0, tiled=True)
    cut = rows * points
    probe_mine = jnp.transpose(payload[:, :cut].reshape(depth_count, rows, points), (1, 0, 2))
    probe_mine = probe_mine.astype(jnp.float32)
    probe_mine = probe_mine.reshape(probe_mine.shape[:2] + (SIDE, SIDE))
    slab_size = probe_count * slab_points
    probe_all = payload[:, cut : cut + slab_size].reshape(depth_count, probe_count, slab_points)
    probe_all = jnp.transpose(probe_all, (1, 0, 2)).reshape(probe_count, -1).astype(jnp.float32)
    parts = payload[:, cut + slab_size :].reshape(depth_count, 3, points).astype(jnp.float32)
    slowness_all = (parts[:, 0] + parts[:, 1]) + parts[:, 2]
    plane_count = slowness_all.shape[0]
    sources = encoded_sources(incident, encode, incident.shape[1])
    sources = sources.reshape(sources.shape[:-1] + (SIDE, SIDE))
    wave_nums = lookup_waves(freq_index, wavenum, wavenum.shape[0])
    spectra = propagator(wave_nums, points_all)
    spectra = spectra.reshape(spectra.shape[:-1] + (SIDE, SIDE))
    spectra_back = conjugate(spectra)
    plane_screens = screens(wave_nums, slowness_all)
    plane_screens = plane_screens.reshape(plane_screens.shape[:-1] + (SIDE, SIDE))
    born_scale = wave_nums * STEP_DEPTH

    fields = [complex_times(plane_screens[:, 0], propagate(sources, spectra, forward, inverse))]

    def born(plane):
        scaled = born_scale[:, None, None, None] * probe_mine[None, :, plane]
        background = fields[plane]
        return jnp.stack([-scaled * background[:, None, 1], scaled * background[:, None, 0]], axis=2)

    tangent = born(0)
    for plane in range(1, plane_count):
        both = jnp.concatenate([fields[-1][:, None], tangent], axis=1)
        moved_on = complex_times(
            plane_screens[:, plane][:, None], propagate(both, spectra[:, None], forward, inverse)
        )
        fields.append(moved_on[:, 0])
        tangent = moved_on[:, 1:] + born(plane)

    adjoint = tangent
    pieces = [None] * plane_count
    for plane in reversed(range(plane_count)):
        background = fields[plane]
        product_terms = born_scale[:, None, None, None] * (
            background[:, None, 0] * adjoint[:, :, 1] - background[:, None, 1] * adjoint[:, :, 0]
        )
        pieces[plane] = jnp.sum(product_terms, axis=0)
        if plane > 0:
            screen = plane_screens[:, plane][:, None]
            turned_back = jnp.stack(
                [
                    screen[..., 0, :, :] * adjoint[..., 0, :, :] + screen[..., 1, :, :] * adjoint[..., 1, :, :],
                    screen[..., 0, :, :] * adjoint[..., 1, :, :] - screen[..., 1, :, :] * adjoint[..., 0, :, :],
                ],
                axis=-3,
            )
            adjoint = propagate(turned_back, spectra_back[:, None], forward, inverse)
    sketch_part = lax.optimization_barrier(jnp.stack(pieces, axis=1))
    rows, planes = sketch_part.shape[0], sketch_part.shape[1]
    by_axes = sketch_part.reshape(rows, planes, CHIPS_Y, CHIPS_Z, CORES, -1)
    slab_width = by_axes.shape[-1]
    by_axes = jnp.transpose(by_axes, (4, 3, 2, 0, 1, 5)).reshape(
        CORES, CHIPS_Z, CHIPS_Y, rows, planes * slab_width
    )
    stage_sizes = [("core", CORES), ("chip_z", CHIPS_Z), ("chip_y", CHIPS_Y)]
    row_total = planes * slab_width * src_count
    sketch_all, gram_matrix = reduce_all(
        by_axes, probe_all, stage_sizes, depth_count, group_count * src_count, row_total
    )
    depth_index = lax.axis_index("depth")
    flattened = lax.dynamic_slice_in_dim(sketch_all, depth_index * slab_width, slab_width, 1)
    local_planes = 1
    lower_factor = lax.linalg.cholesky(gram_matrix, symmetrize_input=False)
    sketch_basis = lax.linalg.triangular_solve(
        lower_factor, flattened, left_side=True, lower=True
    ).reshape(probe_count, local_planes, slab_width)
    return (sketch_basis, lower_factor.T)


def solution(mesh):
    src_size, depth_size = mesh.devices.shape
    cut = mesh.devices.reshape(CHIPS_Y, CHIPS_Z, CORES, depth_size)
    fine = Mesh(cut, SRC_AXES + ("depth",))
    in_specs = (
        P(SRC_AXES, None, None, None),
        P(SRC_AXES),
        P(SRC_AXES),
        P(),
        P("depth", None),
        P(None, "depth", None),
    )
    out_specs = (P(None, "depth", SRC_AXES), P())
    return jax.shard_map(shards, mesh=fine, in_specs=in_specs, out_specs=out_specs, check_vma=False)
```
